768 devices in a mesh: row: 16 (over x, y_hi, core), col: 48 (over y_lo, z).
Axes of the slice: x: 4, y: 8 (y_hi: 2, y_lo: 4; y = y_hi * 4 + y_lo), z: 12, core: 2. Of those that a mesh axis runs over, the one named last changes fastest.
Arguments:
- vectors: bfloat16 [16, 196608], P(None, ('row', 'col')), may hold values from -6 to 6
- tiles: bfloat16 [98304, 128, 128], P(('row', 'col')), may hold values from -0.046875 to 0.046875
- tile_rows: int32 [98304], P(('row', 'col')), may hold values from 0 to 95
- tile_cols: int32 [98304], P(('row', 'col')), may hold values from 0 to 95
- tile_count: int32 [768], P(('row', 'col')), may hold values from 32 to 128, as said below
Outputs:
- applied: float32 [16, 196608], P(None, ('row', 'col'))
The draws below stay inside these ranges and needn't reach their ends.
Inputs may be any that keep to these rules, and one draw needn't show every extreme that they name: `tile_count`: each device has between 32 and 128 live slots; some device fills all 128.
All inputs are finite; a program needn't handle non-finite values.
Results may differ from the reference program's by a relative error of at most 0.0003.
Values may be sent and summed in bfloat16 or wider, within the bound.
No kernel may reach another device: no remote copies, remote signals or barrier semaphores. Data moves between devices by JAX's collectives and lax.ppermute only.
A program may use at most 32 MiB of HBM per device.

```python
import jax
import jax.numpy as jnp
from jax import lax

NVEC = 16
TILE = 128
TS = 96
TPD = 128
GROUPS = 768
SLOTS = 98304
NV = 196608
N_ROW = 16
N_COL = 48


def draw_tile_count(key, part):
    count_key, pick_key = jax.random.split(jax.random.fold_in(key, 17))
    lowered = TPD - jax.random.randint(count_key, (GROUPS,), 0, 3 * TPD // 4 + 1)
    fullest = jax.random.randint(pick_key, (), 0, GROUPS)
    return jnp.where(jnp.arange(GROUPS) == fullest, TPD, lowered).astype(jnp.int32)


def with_ends(values, stream_key, smallest, top_value):
    dims = values.shape
    place = [jax.random.randint(jax.random.fold_in(stream_key, axis), (), 0, dims[axis]) for axis in range(len(dims))]
    values = values.at[tuple(place)].set(smallest)
    longest = dims.index(max(dims))
    place[longest] = (place[longest] + 1) % dims[longest]
    return values.at[tuple(place)].set(top_value)


def block_levels(key, shape, shards, least, high):
    def one(dim, blocks):
        draws = jax.random.uniform(jax.random.fold_in(jax.random.fold_in(key, 6), dim), (blocks,), jnp.float32, least / len(shards), high / len(shards))
        return jnp.repeat(jnp.exp(draws), shape[dim] // blocks).reshape((-1,) + (1,) * (len(shape) - dim - 1))

    loudness = one(*shards[0])
    for cut in shards[1:]:
        loudness = loudness * one(*cut)
    return loudness


def bell_draw(rng, extent, width, bound, cuts=(), kind=jnp.bfloat16):
    array = jax.random.normal(rng, extent, jnp.float32) * width
    if len(cuts) > 0:
        array = block_levels(rng, extent, cuts, -0.22, 0.18) * array
    return jnp.clip(array, min=-bound, max=bound).astype(kind)


def setup_inputs(seed: int = 0) -> dict:
    streams_of = jax.random.split(jax.random.key(seed), 6)
    vectors = bell_draw(streams_of[0], (NVEC, NV), 1.0, 6.0, ((1, 768),))
    tiles = bell_draw(streams_of[1], (SLOTS, TILE, TILE), (TILE * TPD) ** -0.5, 0.046875, ((0, 768),))
    tile_rows = with_ends(jax.random.randint(streams_of[2], (SLOTS,), 0, TS), jax.random.fold_in(streams_of[2], 1), 0, TS - 1).astype(jnp.int32)
    tile_cols = with_ends(jax.random.randint(streams_of[3], (SLOTS,), 0, TS), jax.random.fold_in(streams_of[3], 1), 0, TS - 1).astype(jnp.int32)
    tile_count = draw_tile_count(jax.random.fold_in(streams_of[5], 71), 0)
    return dict(vectors=vectors, tiles=tiles, tile_rows=tile_rows, tile_cols=tile_cols, tile_count=tile_count)


def reference(vectors, tiles, tile_rows, tile_cols, tile_count):
    groups = N_ROW * N_COL
    xblocks = jnp.transpose(vectors.reshape(NVEC, N_ROW * TS, TILE), (1, 0, 2)).astype(jnp.float32)
    tile_sets = tiles.reshape(groups, TPD, TILE, TILE)
    row_sets = tile_rows.reshape(groups, TPD)
    col_sets = tile_cols.reshape(groups, TPD)

    def add_group(accum_rows, entries):
        group_id, tile_set, row_tiles, col_tiles, live_count = entries
        row_seg = group_id // N_COL
        col_seg = (group_id % N_COL) % N_ROW
        glob_rows = (row_seg * TS + row_tiles).astype(jnp.int32)
        glob_cols = (col_seg * TS + col_tiles).astype(jnp.int32)
        live_slots = jnp.arange(TPD, dtype=jnp.int32) < live_count
        mirrored = live_slots & (glob_rows != glob_cols)
        tile_values = tile_set.astype(jnp.float32)
        col_vectors = jnp.take(xblocks, glob_cols, axis=0)
        row_vectors = jnp.take(xblocks, glob_rows, axis=0)
        plain_terms = jnp.einsum("kvj,kij->kvi", col_vectors, tile_values)
        mirror_terms = jnp.einsum("kvi,kij->kvj", row_vectors, tile_values)
        plain_terms = jnp.where(live_slots[:, None, None], plain_terms, 0.0)
        mirror_terms = jnp.where(mirrored[:, None, None], mirror_terms, 0.0)
        accum_rows = accum_rows.at[glob_rows].add(plain_terms).at[glob_cols].add(mirror_terms)
        return accum_rows, None

    start = jnp.zeros((N_ROW * TS, NVEC, TILE), jnp.float32)
    group_ids = jnp.arange(groups, dtype=jnp.int32)
    accum_rows, _ = lax.scan(add_group, start, (group_ids, tile_sets, row_sets, col_sets, tile_count))
    return jnp.transpose(accum_rows, (1, 0, 2)).reshape(NVEC, N_ROW * TS * TILE)
```

```python
import functools

import jax
import jax.numpy as jnp
from jax import lax
from jax.experimental import pallas as pl
from jax.experimental.pallas import tpu as pltpu
from jax.sharding import Mesh, PartitionSpec as P

CHUNK = 16


def product_kernel(mirror, halves, meta, rows, cols, *refs):
    if halves:
        mine, theirs, tiles, out, x, acc, held, sems = refs
    else:
        own, tiles, keep, give, x, acc, held, sems = refs
    slots, width = tiles.shape[0], tiles.shape[1]
    chunks = slots // CHUNK

    def copy(step):
        part = pl.ds(step * CHUNK, CHUNK)
        return pltpu.make_async_copy(tiles.at[part], held.at[part], sems.at[step])

    for step in range(chunks):
        copy(step).start()
    count, core, diagonal = meta[0], meta[1], meta[2]
    if halves:
        half = mine.shape[0]
        for s in range(2):
            lanes = slice(s * width, (s + 1) * width)
            x[pl.ds(core * half, half), s] = mine[:, :, lanes]
            x[pl.ds((1 - core) * half, half), s] = theirs[:, :, lanes]
    else:
        for s in range(2):
            x[:, s] = own[:, :, s * width : (s + 1) * width]
    acc[...] = jnp.zeros_like(acc)

    def step_body(step, carry):
        copy(step).wait()

        @pl.when(step * CHUNK < count)
        def _():
            found = []
            for u in range(CHUNK):
                k = step * CHUNK + u
                row, col = rows[k], cols[k]
                live = k < count
                if mirror:
                    source, target = row, col
                    live = live & ((diagonal == 0) | (row != col))
                    contract = 0
                else:
                    source, target = col, row
                    contract = 1
                picked = x[source // 2, source % 2]
                picked = jnp.where(live, picked, jnp.zeros_like(picked))
                found.append(
                    (
                        target,
                        lax.dot_general(
                            picked,
                            held[k],
                            (((1,), (contract,)), ((), ())),
                            preferred_element_type=jnp.float32,
                        ),
                    )
                )
            for target, part in found:
                acc[target // 2, target % 2] += part

        return carry

    lax.fori_loop(0, chunks, step_body, 0)
    if halves:
        for s in range(2):
            out[:, :, s * width : (s + 1) * width] = acc[:, s]
    else:
        half = keep.shape[0]
        for s in range(2):
            lanes = slice(s * width, (s + 1) * width)
            keep[:, :, lanes] = acc[pl.ds(core * half, half), s]
            give[:, :, lanes] = acc[pl.ds((1 - core) * half, half), s]


def products(mirror, meta, rows, cols, segment, tiles):
    vmem = pl.BlockSpec(memory_space=pltpu.VMEM)
    smem = pl.BlockSpec(memory_space=pltpu.SMEM)
    halves = len(segment) == 2
    pieces = segment[0].shape[0] * len(segment)
    vecs, wide = segment[0].shape[1:]
    slots, width = tiles.shape[:2]
    if halves:
        shapes = jax.ShapeDtypeStruct((pieces, vecs, wide), jnp.float32)
        outs = vmem
    else:
        shapes = [jax.ShapeDtypeStruct((pieces // 2, vecs, wide), jnp.float32)] * 2
        outs = [vmem, vmem]
    return pl.pallas_call(
        functools.partial(product_kernel, mirror, halves),
        out_shape=shapes,
        in_specs=[smem] * 3 + [vmem] * len(segment) + [pl.BlockSpec(memory_space=pl.ANY)],
        out_specs=outs,
        scratch_shapes=[
            pltpu.VMEM((pieces, 2, vecs, width), jnp.bfloat16),
            pltpu.VMEM((pieces, 2, vecs, width), jnp.float32),
            pltpu.VMEM((slots, width, width), jnp.bfloat16),
            pltpu.SemaphoreType.DMA((slots // CHUNK,)),
        ],
    )(meta, rows, cols, *segment, tiles)


def spread(array, axes):
    size = lax.axis_size(axes)
    return lax.all_to_all(
        jnp.broadcast_to(array[None], (size, *array.shape)), axes, 0, 0, tiled=True
    )


def transposing(n_row, n_col):
    fold, half = n_col // n_row, n_col // 2
    pairs = []
    for r in range(n_row):
        for k in range(n_col):
            core, place = divmod(k, half)
            upper, j = divmod(place, fold)
            pairs.append((r * n_col + k, (upper * 2 + core) * n_col + j * n_row + r))
    return pairs


ALL = ("rr", "core", "j", "m")


def shards(pairs, vectors, tiles, tile_rows, tile_cols, tile_count):
    row_index = lax.axis_index(("rr", "core"))
    core = lax.axis_index("core")
    mirror_index = lax.axis_index("m")
    diagonal = (row_index == mirror_index).astype(jnp.int32)
    meta = jnp.stack([tile_count[0], core.astype(jnp.int32), diagonal])
    swap = [(0, 1), (1, 0)]

    own = spread(vectors, ("j", "m"))
    moved = lax.ppermute(vectors, ALL, pairs)
    mine = spread(moved, ("rr", "j"))
    theirs = lax.ppermute(mine, "core", swap)

    keep, give = products(True, meta, tile_rows, tile_cols, [own], tiles)
    keep = keep + lax.ppermute(give, "core", swap)
    mirror_sum = lax.all_to_all(keep, ("rr", "j"), 0, 0, tiled=True).sum(axis=0)
    mirror_sum = lax.ppermute(mirror_sum, ALL, [(d, s) for s, d in pairs])

    plain = products(False, meta, tile_rows, tile_cols, [mine, theirs], tiles)
    plain_sum = lax.all_to_all(plain, ("j", "m"), 0, 0, tiled=True).sum(axis=0)
    return plain_sum + mirror_sum


def solution(mesh):
    n_row, n_col = mesh.shape["row"], mesh.shape["col"]
    fine = Mesh(mesh.devices.reshape(n_row // 2, 2, n_col // n_row, n_row), ALL)
    pairs = transposing(n_row, n_col)
    return jax.shard_map(
        functools.partial(shards, pairs),
        mesh=fine,
        in_specs=(P(None, ALL), P(ALL, None, None), P(ALL), P(ALL), P(ALL)),
        out_specs=P(None, ALL),
        check_vma=False,
    )
```

```python
import functools

import jax
import jax.numpy as jnp
from jax import lax
from jax.experimental import pallas as pl
from jax.experimental.pallas import tpu as pltpu
from jax.sharding import Mesh, PartitionSpec as P

CHUNK = 16
TOP = 14
ALL = ("rr", "core", "j", "m")


def vmem():
    return pl.BlockSpec(memory_space=pltpu.VMEM)


def powers(exponent):
    low = exponent >> 1
    return (
        jnp.exp2(low.astype(jnp.float32)),
        jnp.exp2((exponent - low).astype(jnp.float32)),
    )


def pack(left, right, payload, p):
    rows, width = left.shape
    half = rows // 2
    peak = jnp.max(jnp.maximum(jnp.abs(left), jnp.abs(right)), axis=1, keepdims=True)
    peak = jnp.maximum(peak, 1.2e-38)
    exponent = jnp.floor(jnp.log2(peak)).astype(jnp.int32)
    first, second = powers(TOP - exponent)
    for s, part in enumerate((left, right)):
        scaled = jnp.round((part * first) * second)
        scaled = jnp.minimum(jnp.maximum(scaled, -32767.0), 32767.0)
        payload[p, s * rows : (s + 1) * rows] = scaled.astype(jnp.int32).astype(jnp.int16)
    lane = lax.broadcasted_iota(jnp.int32, (half, width), 1)
    both = jnp.where(lane < width // 2, exponent[:half], exponent[half:])
    payload[p, 2 * rows : 2 * rows + half] = both.astype(jnp.int16)


def unpack(payload, p, rows):
    half = rows // 2
    width = payload.shape[-1]
    exponent = payload[p, 2 * rows : 2 * rows + half].astype(jnp.int32) - TOP
    first, second = powers(exponent)

    def spread_out(factor):
        upper = jnp.broadcast_to(factor[:, :1], (half, width))
        lower = jnp.broadcast_to(factor[:, width // 2 : width // 2 + 1], (half, width))
        return jnp.concatenate([upper, lower], axis=0)

    first, second = spread_out(first), spread_out(second)
    return [
        (payload[p, s * rows : (s + 1) * rows].astype(jnp.float32) * first) * second
        for s in range(2)
    ]


def product_kernel(mirror, meta, sources, targets, *refs):
    if mirror:
        own, tiles, keep, give, x, acc, held, sems = refs
        parts = [own]
    else:
        mine, theirs, tiles, payload, x, acc, held, sems = refs
        parts = [mine, theirs]
    slots, width = tiles.shape[0], tiles.shape[1]
    chunks = slots // CHUNK

    def copy(step):
        part = pl.ds(step * CHUNK, CHUNK)
        return pltpu.make_async_copy(tiles.at[part], held.at[part], sems.at[step])

    for step in range(chunks):
        copy(step).start()
    at = 0
    for part in parts:
        size = part.shape[0]
        for s in range(2):
            x[at : at + size, s] = part[:, :, s * width : (s + 1) * width]
        at += size
    x[at] = jnp.zeros(x.shape[1:], x.dtype)
    acc[...] = jnp.zeros_like(acc)
    count = meta[0]

    def step_body(step, carry):
        copy(step).wait()

        @pl.when(step * CHUNK < count)
        def _():
            found = []
            for u in range(CHUNK):
                k = step * CHUNK + u
                source = sources[k]
                found.append(
                    lax.dot_general(
                        x[source // 2, source % 2],
                        held[k],
                        (((1,), (0 if mirror else 1,)), ((), ())),
                        preferred_element_type=jnp.float32,
                    )
                )
            for u in range(CHUNK):
                target = targets[step * CHUNK + u]
                acc[target // 2, target % 2] += found[u]

        return carry

    lax.fori_loop(0, chunks, step_body, 0)
    if mirror:
        half = keep.shape[0]
        keep[...] = acc[:half]
        give[...] = acc[half:]
    else:

        def pack_body(p, carry):
            pack(acc[p, 0], acc[p, 1], payload, p)
            return carry

        lax.fori_loop(0, payload.shape[0], pack_body, 0, unroll=4)


def products(mirror, meta, sources, targets, segment, tiles):
    smem = pl.BlockSpec(memory_space=pltpu.SMEM)
    pieces = segment[0].shape[0] * len(segment)
    vecs = segment[0].shape[1]
    slots, width = tiles.shape[:2]
    if mirror:
        shapes = [jax.ShapeDtypeStruct((pieces // 2, 2, vecs, width), jnp.float32)] * 2
        outs = [vmem(), vmem()]
    else:
        shapes = jax.ShapeDtypeStruct((pieces, 5 * vecs // 2, width), jnp.int16)
        outs = vmem()
    return pl.pallas_call(
        functools.partial(product_kernel, mirror),
        out_shape=shapes,
        in_specs=[smem] * 3 + [vmem()] * len(segment) + [pl.BlockSpec(memory_space=pl.ANY)],
        out_specs=outs,
        scratch_shapes=[
            pltpu.VMEM((pieces + 1, 2, vecs, width), jnp.bfloat16),
            pltpu.VMEM((pieces, 2, vecs, width), jnp.float32),
            pltpu.VMEM((slots, width, width), jnp.bfloat16),
            pltpu.SemaphoreType.DMA((slots // CHUNK,)),
        ],
    )(meta, sources, targets, *segment, tiles)


def join_kernel(keep, came, payload):
    def body(p, carry):
        pack(keep[p, 0] + came[p, 0], keep[p, 1] + came[p, 1], payload, p)
        return carry

    lax.fori_loop(0, payload.shape[0], body, 0, unroll=4)


def join(keep, came):
    pieces, _, vecs, width = keep.shape
    return pl.pallas_call(
        join_kernel,
        out_shape=jax.ShapeDtypeStruct((pieces, 5 * vecs // 2, width), jnp.int16),
        in_specs=[vmem()] * 2,
        out_specs=vmem(),
    )(keep, came)


def total_kernel(kinds, vecs, payload, *refs):
    *added, out = refs
    width = payload.shape[-1]

    for kind in range(kinds):

        def body(i, sums, kind=kind):
            left, right = unpack(payload, i * kinds + kind, vecs)
            return sums[0] + left, sums[1] + right

        zero = jnp.zeros((vecs, width), jnp.float32)
        sums = lax.fori_loop(0, payload.shape[0] // kinds, body, (zero, zero), unroll=4)
        for s in range(2):
            lanes = slice(s * width, (s + 1) * width)
            total = sums[s]
            for other in added:
                total = total + other[:, lanes]
            out[kind, :, lanes] = total


def total(kinds, vecs, payload, *added):
    width = payload.shape[-1]
    return pl.pallas_call(
        functools.partial(total_kernel, kinds, vecs),
        out_shape=jax.ShapeDtypeStruct((kinds, vecs, 2 * width), jnp.float32),
        in_specs=[vmem()] * (1 + len(added)),
        out_specs=vmem(),
    )(payload, *added)


def spread(array, axes):
    size = lax.axis_size(axes)
    return lax.all_to_all(
        jnp.broadcast_to(array[None], (size, *array.shape)), axes, 0, 0, tiled=True
    )


def shards(vectors, tiles, tile_rows, tile_cols, tile_count):
    n_row, fold = lax.axis_size("m"), lax.axis_size("j")
    vecs = vectors.shape[0]
    slots = tiles.shape[0]
    row_index = lax.axis_index(("rr", "core"))
    core, j = lax.axis_index("core"), lax.axis_index("j")
    mirror_index = lax.axis_index("m")
    swap = [(0, 1), (1, 0)]
    shift = lambda k: [(i, (i + k) % fold) for i in range(fold)]
    turn = [
        ((r * fold + i) * n_row + a, (a * fold + i) * n_row + r)
        for r in range(n_row)
        for i in range(fold)
        for a in range(n_row)
    ]

    shard, half = tile_cols // 2, tile_cols % 2
    member = shard % n_row
    behind = (j - shard // n_row) % fold
    place = ((member % 2) ^ core) * (n_row // 2) + member // 2
    col_place = (place * fold + behind) * 2 + half
    nothing = 2 * n_row * fold
    live = jnp.arange(slots, dtype=jnp.int32) < tile_count[0]
    mirrored = live & ((row_index != mirror_index) | (tile_rows != tile_cols))
    mirror_source = jnp.where(mirrored, tile_rows, nothing)
    plain_source = jnp.where(live, col_place, nothing)

    own = spread(vectors, ("j", "m"))
    trio = jnp.stack([vectors] + [lax.ppermute(vectors, "j", shift(k)) for k in range(1, fold)])
    trio = lax.ppermute(trio, ALL, turn)
    own, trio = lax.optimization_barrier((own, trio))
    mine = spread(trio, "rr").reshape(-1, *vectors.shape)
    theirs = lax.ppermute(mine, "core", swap)

    keep, give = products(True, tile_count, mirror_source, col_place, [own], tiles)
    sums = join(keep, lax.ppermute(give, "core", swap))
    sums = lax.all_to_all(sums, "rr", 0, 0, tiled=True)
    sums = lax.ppermute(total(fold, vecs, sums), ALL, turn)
    mirror_sums = [sums[0]] + [lax.ppermute(sums[k], "j", shift(-k)) for k in range(1, fold)]

    plain = products(False, tile_count, plain_source, tile_rows, [mine, theirs], tiles)
    plain = lax.all_to_all(plain, ("j", "m"), 0, 0, tiled=True)
    return total(1, vecs, plain, *mirror_sums)[0]


def solution(mesh):
    n_row, n_col = mesh.shape["row"], mesh.shape["col"]
    fine = Mesh(mesh.devices.reshape(n_row // 2, 2, n_col // n_row, n_row), ALL)

    return jax.shard_map(
        shards,
        mesh=fine,
        in_specs=(P(None, ALL), P(ALL, None, None), P(ALL), P(ALL), P(ALL)),
        out_specs=P(None, ALL),
        check_vma=False,
    )
```

```python
import functools

import jax
import jax.numpy as jnp
from jax import lax
from jax.experimental import pallas as pl
from jax.experimental.pallas import tpu as pltpu
from jax.sharding import Mesh, PartitionSpec as P

CHUNK = 16
TOP = 14
ALL = ("rr", "core", "j", "m")


def vmem():
    return pl.BlockSpec(memory_space=pltpu.VMEM)


def powers(exponent):
    low = exponent >> 1
    return (
        jnp.exp2(low.astype(jnp.float32)),
        jnp.exp2((exponent - low).astype(jnp.float32)),
    )


def pack(left, right, payload, p):
    rows, width = left.shape
    half = rows // 2
    peak = jnp.max(jnp.maximum(jnp.abs(left), jnp.abs(right)), axis=1, keepdims=True)
    peak = jnp.maximum(peak, 1.2e-38)
    exponent = jnp.floor(jnp.log2(peak)).astype(jnp.int32)
    first, second = powers(TOP - exponent)
    for s, part in enumerate((left, right)):
        scaled = jnp.round((part * first) * second)
        scaled = jnp.minimum(jnp.maximum(scaled, -32767.0), 32767.0)
        payload[p, s * rows : (s + 1) * rows] = scaled.astype(jnp.int32).astype(jnp.int16)
    lane = lax.broadcasted_iota(jnp.int32, (half, width), 1)
    both = jnp.where(lane < width // 2, exponent[:half], exponent[half:])
    payload[p, 2 * rows : 2 * rows + half] = both.astype(jnp.int16)


def unpack(payload, p, rows):
    half = rows // 2
    width = payload.shape[-1]
    exponent = payload[p, 2 * rows : 2 * rows + half].astype(jnp.int32) - TOP
    first, second = powers(exponent)

    def spread_out(factor):
        upper = jnp.broadcast_to(factor[:, :1], (half, width))
        lower = jnp.broadcast_to(factor[:, width // 2 : width // 2 + 1], (half, width))
        return jnp.concatenate([upper, lower], axis=0)

    first, second = spread_out(first), spread_out(second)
    return [
        (payload[p, s * rows : (s + 1) * rows].astype(jnp.float32) * first) * second
        for s in range(2)
    ]


def product_kernel(mirror, meta, sources, targets, *refs):
    if mirror:
        own, tiles, keep, give, x, acc, held, sems = refs
        parts = [own]
    else:
        mine, theirs, tiles, acc, x, held, sems = refs
        parts = [mine, theirs]
    slots, width = tiles.shape[0], tiles.shape[1]
    chunks = slots // CHUNK

    def copy(step):
        part = pl.ds(step * CHUNK, CHUNK)
        return pltpu.make_async_copy(tiles.at[part], held.at[part], sems.at[step])

    for step in range(chunks):
        copy(step).start()
    at = 0
    for part in parts:
        size = part.shape[0]
        for s in range(2):
            x[at : at + size, s] = part[:, :, s * width : (s + 1) * width]
        at += size
    x[at] = jnp.zeros(x.shape[1:], x.dtype)
    acc[...] = jnp.zeros_like(acc)
    count = meta[0]

    def step_body(step, carry):
        copy(step).wait()

        @pl.when(step * CHUNK < count)
        def _():
            found = []
            for u in range(CHUNK):
                k = step * CHUNK + u
                source = sources[k]
                found.append(
                    lax.dot_general(
                        x[source // 2, source % 2],
                        held[k],
                        (((1,), (0 if mirror else 1,)), ((), ())),
                        preferred_element_type=jnp.float32,
                    )
                )
            for u in range(CHUNK):
                target = targets[step * CHUNK + u]
                acc[target // 2, target % 2] += found[u]

        return carry

    lax.fori_loop(0, chunks, step_body, 0)
    if mirror:
        half = keep.shape[0]
        keep[...] = acc[:half]
        give[...] = acc[half:]


def products(mirror, meta, sources, targets, segment, tiles):
    smem = pl.BlockSpec(memory_space=pltpu.SMEM)
    pieces = segment[0].shape[0] * len(segment)
    vecs = segment[0].shape[1]
    slots, width = tiles.shape[:2]
    scratch = [
        pltpu.VMEM((pieces + 1, 2, vecs, width), jnp.bfloat16),
        pltpu.VMEM((pieces, 2, vecs, width), jnp.float32),
        pltpu.VMEM((slots, width, width), jnp.bfloat16),
        pltpu.SemaphoreType.DMA((slots // CHUNK,)),
    ]
    if mirror:
        shapes = [jax.ShapeDtypeStruct((pieces // 2, 2, vecs, width), jnp.float32)] * 2
        outs = [vmem(), vmem()]
    else:
        shapes = jax.ShapeDtypeStruct((pieces, 2, vecs, width), jnp.float32)
        outs = vmem()
        del scratch[1]
    return pl.pallas_call(
        functools.partial(product_kernel, mirror),
        out_shape=shapes,
        in_specs=[smem] * 3 + [vmem()] * len(segment) + [pl.BlockSpec(memory_space=pl.ANY)],
        out_specs=outs,
        scratch_shapes=scratch,
    )(meta, sources, targets, *segment, tiles)


def join_kernel(keep, came, payload):
    def body(p, carry):
        pack(keep[p, 0] + came[p, 0], keep[p, 1] + came[p, 1], payload, p)
        return carry

    lax.fori_loop(0, payload.shape[0], body, 0, unroll=4)


def join(keep, came):
    pieces, _, vecs, width = keep.shape
    return pl.pallas_call(
        join_kernel,
        out_shape=jax.ShapeDtypeStruct((pieces, 5 * vecs // 2, width), jnp.int16),
        in_specs=[vmem()] * 2,
        out_specs=vmem(),
    )(keep, came)


def merge_kernel(place, sums, trio, payload):
    pieces, _, _, width = sums.shape
    fold = trio.shape[0]
    step = pieces // fold

    def body(p, carry):
        pack(sums[p, 0], sums[p, 1], payload, p)
        return carry

    lax.fori_loop(0, pieces, body, 0, unroll=4)
    for i in range(fold):
        p = i * step + place[0]
        pack(
            sums[p, 0] + trio[i, :, :width],
            sums[p, 1] + trio[i, :, width:],
            payload,
            p,
        )


def merge(place, sums, trio):
    pieces, _, vecs, width = sums.shape
    return pl.pallas_call(
        merge_kernel,
        out_shape=jax.ShapeDtypeStruct((pieces, 5 * vecs // 2, width), jnp.int16),
        in_specs=[pl.BlockSpec(memory_space=pltpu.SMEM)] + [vmem()] * 2,
        out_specs=vmem(),
    )(place, sums, trio)


def total_kernel(kinds, vecs, payload, out):
    width = payload.shape[-1]

    for kind in range(kinds):

        def body(i, sums, kind=kind):
            left, right = unpack(payload, i * kinds + kind, vecs)
            return sums[0] + left, sums[1] + right

        zero = jnp.zeros((vecs, width), jnp.float32)
        sums = lax.fori_loop(0, payload.shape[0] // kinds, body, (zero, zero), unroll=4)
        for s in range(2):
            out[kind, :, s * width : (s + 1) * width] = sums[s]


def total(kinds, vecs, payload):
    width = payload.shape[-1]
    return pl.pallas_call(
        functools.partial(total_kernel, kinds, vecs),
        out_shape=jax.ShapeDtypeStruct((kinds, vecs, 2 * width), jnp.float32),
        in_specs=[vmem()],
        out_specs=vmem(),
    )(payload)


def spread(array, axes):
    size = lax.axis_size(axes)
    return lax.all_to_all(
        jnp.broadcast_to(array[None], (size, *array.shape)), axes, 0, 0, tiled=True
    )


def shards(vectors, tiles, tile_rows, tile_cols, tile_count):
    n_row, fold = lax.axis_size("m"), lax.axis_size("j")
    vecs = vectors.shape[0]
    slots = tiles.shape[0]
    row_index = lax.axis_index(("rr", "core"))
    core = lax.axis_index("core")
    mirror_index = lax.axis_index("m")
    swap = [(0, 1), (1, 0)]
    turn = [
        ((r * fold + i) * n_row + a, (a * fold + i) * n_row + r)
        for r in range(n_row)
        for i in range(fold)
        for a in range(n_row)
    ]

    shard, half = tile_cols // 2, tile_cols % 2
    member = shard % n_row
    place = ((member % 2) ^ core) * (n_row // 2) + member // 2
    col_place = (place * fold + shard // n_row) * 2 + half
    nothing = 2 * n_row * fold
    live = jnp.arange(slots, dtype=jnp.int32) < tile_count[0]
    mirrored = live & ((row_index != mirror_index) | (tile_rows != tile_cols))
    mirror_source = jnp.where(mirrored, tile_rows, nothing)
    plain_source = jnp.where(live, col_place, nothing)

    own = spread(vectors, ("j", "m"))
    trio = own.reshape(fold, n_row, *vectors.shape)
    trio = lax.dynamic_index_in_dim(trio, mirror_index, 1, keepdims=False)
    trio = lax.ppermute(trio, ALL, turn)
    keep, give = products(True, tile_count, mirror_source, col_place, [own], tiles)
    came = lax.ppermute(give, "core", swap)
    sums = join(keep, came)
    sums = lax.all_to_all(sums, "rr", 0, 0, tiled=True)
    sums = total(fold, vecs, sums)
    sums = lax.ppermute(sums, ALL, turn)

    mine = spread(trio, "rr").reshape(-1, *vectors.shape)
    theirs = lax.ppermute(mine, "core", swap)
    plain = products(False, tile_count, plain_source, tile_rows, [mine, theirs], tiles)
    plain = merge(mirror_index[None].astype(jnp.int32), plain, sums)
    plain = lax.all_to_all(plain, ("j", "m"), 0, 0, tiled=True)
    return total(1, vecs, plain)[0]


def solution(mesh):
    n_row, n_col = mesh.shape["row"], mesh.shape["col"]
    fine = Mesh(mesh.devices.reshape(n_row // 2, 2, n_col // n_row, n_row), ALL)

    return jax.shard_map(
        shards,
        mesh=fine,
        in_specs=(P(None, ALL), P(ALL, None, None), P(ALL), P(ALL), P(ALL)),
        out_specs=P(None, ALL),
        check_vma=False,
    )
```

```python
import functools

import jax
import jax.numpy as jnp
from jax import lax
from jax.experimental import pallas as pl
from jax.experimental.pallas import tpu as pltpu
from jax.sharding import PartitionSpec as P

CHUNK = 16
TOP = 14


def vmem():
    return pl.BlockSpec(memory_space=pltpu.VMEM)


def powers(exponent):
    low = exponent >> 1
    return (
        jnp.exp2(low.astype(jnp.float32)),
        jnp.exp2((exponent - low).astype(jnp.float32)),
    )


def pack(left, right, payload, p):
    rows, width = left.shape
    half = rows // 2
    peak = jnp.max(jnp.maximum(jnp.abs(left), jnp.abs(right)), axis=1, keepdims=True)
    peak = jnp.maximum(peak, 1.2e-38)
    exponent = jnp.floor(jnp.log2(peak)).astype(jnp.int32)
    first, second = powers(TOP - exponent)
    for s, part in enumerate((left, right)):
        scaled = jnp.round((part * first) * second)
        scaled = jnp.minimum(jnp.maximum(scaled, -32767.0), 32767.0)
        payload[p, s * rows : (s + 1) * rows] = scaled.astype(jnp.int32).astype(jnp.int16)
    lane = lax.broadcasted_iota(jnp.int32, (half, width), 1)
    both = jnp.where(lane < width // 2, exponent[:half], exponent[half:])
    payload[p, 2 * rows : 2 * rows + half] = both.astype(jnp.int16)


def unpack(payload, p, rows):
    half = rows // 2
    width = payload.shape[-1]
    exponent = payload[p, 2 * rows : 2 * rows + half].astype(jnp.int32) - TOP
    first, second = powers(exponent)

    def spread_out(factor):
        upper = jnp.broadcast_to(factor[:, :1], (half, width))
        lower = jnp.broadcast_to(factor[:, width // 2 : width // 2 + 1], (half, width))
        return jnp.concatenate([upper, lower], axis=0)

    first, second = spread_out(first), spread_out(second)
    return [
        (payload[p, s * rows : (s + 1) * rows].astype(jnp.float32) * first) * second
        for s in range(2)
    ]


def product_kernel(mirror, meta, sources, targets, *refs):
    if mirror:
        own, tiles, keep, give, x, acc, held, sems = refs
        parts = [own]
    else:
        mine, theirs, tiles, acc, x, held, sems = refs
        parts = [mine, theirs]
    slots, width = tiles.shape[0], tiles.shape[1]
    chunks = slots // CHUNK

    def copy(step):
        part = pl.ds(step * CHUNK, CHUNK)
        return pltpu.make_async_copy(tiles.at[part], held.at[part], sems.at[step])

    for step in range(chunks):
        copy(step).start()
    at = 0
    for part in parts:
        size = part.shape[0]
        for s in range(2):
            x[at : at + size, s] = part[:, :, s * width : (s + 1) * width]
        at += size
    x[at] = jnp.zeros(x.shape[1:], x.dtype)
    acc[...] = jnp.zeros_like(acc)
    count = meta[0]

    def step_body(step, carry):
        copy(step).wait()

        @pl.when(step * CHUNK < count)
        def _():
            found = []
            for u in range(CHUNK):
                k = step * CHUNK + u
                source = sources[k]
                found.append(
                    lax.dot_general(
                        x[source // 2, source % 2],
                        held[k],
                        (((1,), (0 if mirror else 1,)), ((), ())),
                        preferred_element_type=jnp.float32,
                    )
                )
            for u in range(CHUNK):
                target = targets[step * CHUNK + u]
                acc[target // 2, target % 2] += found[u]

        return carry

    lax.fori_loop(0, chunks, step_body, 0)
    if mirror:
        half = keep.shape[0]
        keep[...] = acc[:half]
        give[...] = acc[half:]


def products(mirror, meta, sources, targets, segment, tiles):
    smem = pl.BlockSpec(memory_space=pltpu.SMEM)
    pieces = segment[0].shape[0] * len(segment)
    vecs = segment[0].shape[1]
    slots, width = tiles.shape[:2]
    scratch = [
        pltpu.VMEM((pieces + 1, 2, vecs, width), jnp.bfloat16),
        pltpu.VMEM((pieces, 2, vecs, width), jnp.float32),
        pltpu.VMEM((slots, width, width), jnp.bfloat16),
        pltpu.SemaphoreType.DMA((slots // CHUNK,)),
    ]
    if mirror:
        shapes = [jax.ShapeDtypeStruct((pieces // 2, 2, vecs, width), jnp.float32)] * 2
        outs = [vmem(), vmem()]
    else:
        shapes = jax.ShapeDtypeStruct((pieces, 2, vecs, width), jnp.float32)
        outs = vmem()
        del scratch[1]
    return pl.pallas_call(
        functools.partial(product_kernel, mirror),
        out_shape=shapes,
        in_specs=[smem] * 3 + [vmem()] * len(segment) + [pl.BlockSpec(memory_space=pl.ANY)],
        out_specs=outs,
        scratch_shapes=scratch,
    )(meta, sources, targets, *segment, tiles)


def join_kernel(keep, came, payload):
    def body(p, carry):
        pack(keep[p, 0] + came[p, 0], keep[p, 1] + came[p, 1], payload, p)
        return carry

    lax.fori_loop(0, payload.shape[0], body, 0, unroll=4)


def join(keep, came):
    pieces, _, vecs, width = keep.shape
    return pl.pallas_call(
        join_kernel,
        out_shape=jax.ShapeDtypeStruct((pieces, 5 * vecs // 2, width), jnp.int16),
        in_specs=[vmem()] * 2,
        out_specs=vmem(),
    )(keep, came)


def merge_kernel(side, sums, came, payload):
    pieces, _, vecs, _ = sums.shape
    half = pieces // 2
    first, other = side[0] * half, (1 - side[0]) * half

    def body(i, carry):
        left, right = unpack(came, i, vecs)
        pack(sums[first + i, 0] + left, sums[first + i, 1] + right, payload, first + i)
        pack(sums[other + i, 0], sums[other + i, 1], payload, other + i)
        return carry

    lax.fori_loop(0, half, body, 0, unroll=2)


def merge(side, sums, came):
    pieces, _, vecs, width = sums.shape
    return pl.pallas_call(
        merge_kernel,
        out_shape=jax.ShapeDtypeStruct((pieces, 5 * vecs // 2, width), jnp.int16),
        in_specs=[pl.BlockSpec(memory_space=pltpu.SMEM)] + [vmem()] * 2,
        out_specs=vmem(),
    )(side, sums, came)


def total_kernel(vecs, payload, out):
    width = payload.shape[-1]

    def body(i, sums):
        left, right = unpack(payload, i, vecs)
        return sums[0] + left, sums[1] + right

    zero = jnp.zeros((vecs, width), jnp.float32)
    sums = lax.fori_loop(0, payload.shape[0], body, (zero, zero), unroll=4)
    for s in range(2):
        out[:, s * width : (s + 1) * width] = sums[s]


def total(vecs, payload):
    return pl.pallas_call(
        functools.partial(total_kernel, vecs),
        out_shape=jax.ShapeDtypeStruct((vecs, 2 * payload.shape[-1]), jnp.float32),
        in_specs=[vmem()],
        out_specs=vmem(),
    )(payload)


def assign(cost):
    n = len(cost)
    row_price, col_price = [0] * (n + 1), [0] * (n + 1)
    owner, trail = [0] * (n + 1), [0] * (n + 1)
    for i in range(1, n + 1):
        owner[0], at = i, 0
        slack, seen = [float("inf")] * (n + 1), [False] * (n + 1)
        while owner[at]:
            seen[at] = True
            row, gap, nearest = owner[at], float("inf"), 0
            for c in range(1, n + 1):
                if not seen[c]:
                    left = cost[row - 1][c - 1] - row_price[row] - col_price[c]
                    if left < slack[c]:
                        slack[c], trail[c] = left, at
                    if slack[c] < gap:
                        gap, nearest = slack[c], c
            for c in range(n + 1):
                if seen[c]:
                    row_price[owner[c]] += gap
                    col_price[c] -= gap
                else:
                    slack[c] -= gap
            at = nearest
        while at:
            owner[at] = owner[trail[at]]
            at = trail[at]
    columns = [0] * n
    for c in range(1, n + 1):
        columns[owner[c] - 1] = c - 1
    return columns


def position(row, col, n_col):
    deep = n_col // 4
    return row // 4, (row // 2) % 2 * 4 + col // deep, col % deep


def hops(one, other, sides=(4, 8, 12)):
    return [min((p - q) % side, (q - p) % side) for p, q, side in zip(one, other, sides)]


def handing(n_row, n_col):
    pairs = []
    for m in range(n_row):
        takers = [(r, c) for c in range(m, n_col, n_row) for r in range(n_row)]
        cost = []
        for c in range(n_col):
            start = position(m, c, n_col)
            line = []
            for r, col in takers:
                far = sum(h * h + 4 * h for h in hops(start, position(r, col, n_col)))
                line.append(far + (100000 if r % 2 != c % 2 else 0))
            cost.append(line)
        for c, taker in enumerate(assign(cost)):
            r, col = takers[taker]
            pairs.append((m * n_col + c, r * n_col + col))
    return pairs


def spread(array, axes):
    size = lax.axis_size(axes)
    return lax.all_to_all(
        jnp.broadcast_to(array[None], (size, *array.shape)), axes, 0, 0, tiled=True
    )


def shards(pairs, vectors, tiles, tile_rows, tile_cols, tile_count):
    axes = ("row", "col")
    n_row, n_col = lax.axis_size("row"), lax.axis_size("col")
    vecs, slots = vectors.shape[0], tiles.shape[0]
    pieces = n_col // 2
    row_index, col_index = lax.axis_index("row"), lax.axis_index("col")
    core, side = row_index % 2, col_index % 2
    swap = [(r, r ^ 1) for r in range(n_row)]

    col_place = ((tile_cols // n_col) ^ core) * n_col + tile_cols % n_col
    nothing = 2 * n_col
    live = jnp.arange(slots, dtype=jnp.int32) < tile_count[0]
    mirrored = live & ((row_index != col_index % n_row) | (tile_rows != tile_cols))
    mirror_source = jnp.where(mirrored, tile_rows, nothing)
    plain_source = jnp.where(live, col_place, nothing)

    own = spread(vectors, "col")
    mine = lax.dynamic_slice_in_dim(own, side * pieces, pieces, 0)
    mine = lax.ppermute(mine, axes, pairs)
    keep, give = products(True, tile_count, mirror_source, col_place, [own], tiles)
    came = lax.ppermute(give, "row", swap)
    sums = join(keep, came)
    sums = lax.ppermute(sums, axes, [(taker, giver) for giver, taker in pairs])

    theirs = lax.ppermute(mine, "row", swap)
    plain = products(False, tile_count, plain_source, tile_rows, [mine, theirs], tiles)
    plain = merge(side[None].astype(jnp.int32), plain, sums)
    plain = lax.all_to_all(plain, "col", 0, 0, tiled=True)
    return total(vecs, plain)


def solution(mesh):
    pairs = handing(mesh.shape["row"], mesh.shape["col"])

    def step(*args):
        return shards(pairs, *args)

    both = ("row", "col")
    return jax.shard_map(
        step,
        mesh=mesh,
        in_specs=(P(None, both), P(both, None, None), P(both), P(both), P(both)),
        out_specs=P(None, both),
        check_vma=False,
    )
```

```python
import functools

import jax
import jax.numpy as jnp
from jax import lax
from jax.experimental import pallas as pl
from jax.experimental.pallas import tpu as pltpu
from jax.sharding import PartitionSpec as P

CHUNK = 16
GROUP = 8
TOP = 14


def grant(mib):
    return pltpu.CompilerParams(vmem_limit_bytes=mib * 2**20)


def vmem():
    return pl.BlockSpec(memory_space=pltpu.VMEM)


def powers(exponent):
    low = exponent >> 1
    return (
        jnp.exp2(low.astype(jnp.float32)),
        jnp.exp2((exponent - low).astype(jnp.float32)),
    )


def pack(sums, payload, at):
    group, _, rows, width = sums.shape
    half = rows // 2
    peak = jnp.max(jnp.max(jnp.abs(sums), axis=1), axis=-1, keepdims=True)
    peak = jnp.maximum(peak, 1.2e-38)
    exponent = jnp.floor(jnp.log2(peak)).astype(jnp.int32)
    first, second = powers(TOP - exponent)
    for s in range(2):
        scaled = jnp.round((sums[:, s] * first) * second)
        scaled = jnp.minimum(jnp.maximum(scaled, -32767.0), 32767.0)
        scaled = scaled.astype(jnp.int32).astype(jnp.int16)
        payload[pl.ds(at, group), s * rows : (s + 1) * rows] = scaled
    lane = lax.broadcasted_iota(jnp.int32, (group, half, width), 2)
    both = jnp.where(lane < width // 2, exponent[:, :half], exponent[:, half:])
    payload[pl.ds(at, group), 2 * rows : 2 * rows + half] = both.astype(jnp.int16)


def unpack(payload, at, group, rows):
    half = rows // 2
    width = payload.shape[-1]
    exponent = payload[pl.ds(at, group), 2 * rows : 2 * rows + half].astype(jnp.int32)
    factors = []
    for factor in powers(exponent - TOP):
        upper = jnp.broadcast_to(factor[:, :, :1], (group, half, width))
        lower = factor[:, :, width // 2 : width // 2 + 1]
        lower = jnp.broadcast_to(lower, (group, half, width))
        factors.append(jnp.concatenate([upper, lower], axis=1))
    parts = [payload[pl.ds(at, group), s * rows : (s + 1) * rows] for s in range(2)]
    return [(part.astype(jnp.float32) * factors[0]) * factors[1] for part in parts]


def product_kernel(mirror, meta, sources, targets, *refs):
    if mirror:
        own, tiles, keep, give, x, held, sems, acc = refs
        parts = [own]
    else:
        mine, theirs, tiles, acc, x, held, sems = refs
        parts = [mine, theirs]
    width = tiles.shape[1]
    chunks = tiles.shape[0] // CHUNK

    def copy(step):
        part = pl.ds(step * CHUNK, CHUNK)
        return pltpu.make_async_copy(tiles.at[part], held.at[part], sems.at[step])

    for step in range(chunks):
        copy(step).start()
    at = 0
    for part in parts:
        size = part.shape[0]
        for s in range(2):
            x[at : at + size, s] = part[:, :, s * width : (s + 1) * width]
        at += size
    x[at] = jnp.zeros(x.shape[1:], x.dtype)
    acc[...] = jnp.zeros_like(acc)

    def step_body(step, carry):
        copy(step).wait()

        @pl.when(step * CHUNK < meta[0])
        def _():
            found = []
            for u in range(CHUNK):
                k = step * CHUNK + u
                source = sources[k]
                found.append(
                    lax.dot_general(
                        x[source // 2, source % 2],
                        held[k],
                        (((1,), (0 if mirror else 1,)), ((), ())),
                        preferred_element_type=jnp.float32,
                    )
                )
            for u in range(CHUNK):
                target = targets[step * CHUNK + u]
                acc[target // 2, target % 2] += found[u]

        return carry

    lax.fori_loop(0, chunks, step_body, 0)
    if mirror:
        half = keep.shape[0]
        keep[...] = acc[:half]
        give[...] = acc[half:]


def products(mirror, meta, sources, targets, segment, tiles):
    smem = pl.BlockSpec(memory_space=pltpu.SMEM)
    pieces = segment[0].shape[0] * len(segment)
    vecs = segment[0].shape[1]
    width = tiles.shape[1]
    scratch = [
        pltpu.VMEM((pieces + 1, 2, vecs, width), jnp.bfloat16),
        pltpu.VMEM(tiles.shape, tiles.dtype),
        pltpu.SemaphoreType.DMA((tiles.shape[0] // CHUNK,)),
    ]
    if mirror:
        shapes = [jax.ShapeDtypeStruct((pieces // 2, 2, vecs, width), jnp.float32)] * 2
        outs = [vmem(), vmem()]
        scratch.append(pltpu.VMEM((pieces, 2, vecs, width), jnp.float32))
    else:
        shapes = jax.ShapeDtypeStruct((pieces, 2, vecs, width), jnp.float32)
        outs = vmem()
    return pl.pallas_call(
        functools.partial(product_kernel, mirror),
        out_shape=shapes,
        in_specs=[smem] * 3 + [vmem()] * len(segment) + [pl.BlockSpec(memory_space=pl.ANY)],
        out_specs=outs,
        scratch_shapes=scratch,
        compiler_params=grant(12),
    )(meta, sources, targets, *segment, tiles)


def join_kernel(keep, came, payload):
    def body(i, carry):
        part = pl.ds(i * GROUP, GROUP)
        pack(keep[part] + came[part], payload, i * GROUP)
        return carry

    lax.fori_loop(0, payload.shape[0] // GROUP, body, 0)


def join(keep, came):
    pieces, _, vecs, width = keep.shape
    return pl.pallas_call(
        join_kernel,
        out_shape=jax.ShapeDtypeStruct((pieces, 5 * vecs // 2, width), jnp.int16),
        in_specs=[vmem()] * 2,
        out_specs=vmem(),
        compiler_params=grant(4),
    )(keep, came)


def merge_kernel(side, sums, came, payload):
    pieces, _, vecs, _ = sums.shape
    half = pieces // 2
    first, other = side[0] * half, (1 - side[0]) * half

    def body(i, carry):
        at = i * GROUP
        added = jnp.stack(unpack(came, at, GROUP, vecs), axis=1)
        pack(sums[pl.ds(first + at, GROUP)] + added, payload, first + at)
        pack(sums[pl.ds(other + at, GROUP)], payload, other + at)
        return carry

    lax.fori_loop(0, half // GROUP, body, 0)


def merge(side, sums, came):
    pieces, _, vecs, width = sums.shape
    return pl.pallas_call(
        merge_kernel,
        out_shape=jax.ShapeDtypeStruct((pieces, 5 * vecs // 2, width), jnp.int16),
        in_specs=[pl.BlockSpec(memory_space=pltpu.SMEM)] + [vmem()] * 2,
        out_specs=vmem(),
        compiler_params=grant(4),
    )(side, sums, came)


def total_kernel(vecs, payload, out):
    width = payload.shape[-1]

    def body(i, sums):
        parts = unpack(payload, i * GROUP, GROUP, vecs)
        return tuple(one + part.sum(axis=0) for one, part in zip(sums, parts))

    zero = jnp.zeros((vecs, width), jnp.float32)
    sums = lax.fori_loop(0, payload.shape[0] // GROUP, body, (zero, zero))
    for s in range(2):
        out[:, s * width : (s + 1) * width] = sums[s]


def total(vecs, payload):
    return pl.pallas_call(
        functools.partial(total_kernel, vecs),
        out_shape=jax.ShapeDtypeStruct((vecs, 2 * payload.shape[-1]), jnp.float32),
        in_specs=[vmem()],
        out_specs=vmem(),
        compiler_params=grant(4),
    )(payload)


def assign(cost):
    n = len(cost)
    row_price, col_price = [0] * (n + 1), [0] * (n + 1)
    owner, trail = [0] * (n + 1), [0] * (n + 1)
    for i in range(1, n + 1):
        owner[0], at = i, 0
        slack, seen = [float("inf")] * (n + 1), [False] * (n + 1)
        while owner[at]:
            seen[at] = True
            row, gap, nearest = owner[at], float("inf"), 0
            for c in range(1, n + 1):
                if not seen[c]:
                    left = cost[row - 1][c - 1] - row_price[row] - col_price[c]
                    if left < slack[c]:
                        slack[c], trail[c] = left, at
                    if slack[c] < gap:
                        gap, nearest = slack[c], c
            for c in range(n + 1):
                if seen[c]:
                    row_price[owner[c]] += gap
                    col_price[c] -= gap
                else:
                    slack[c] -= gap
            at = nearest
        while at:
            owner[at] = owner[trail[at]]
            at = trail[at]
    columns = [0] * n
    for c in range(1, n + 1):
        columns[owner[c] - 1] = c - 1
    return columns


def position(row, col, n_col):
    deep = n_col // 4
    return row // 4, (row // 2) % 2 * 4 + col // deep, col % deep


def hops(one, other, sides=(4, 8, 12)):
    return [min((p - q) % side, (q - p) % side) for p, q, side in zip(one, other, sides)]


def handing(n_row, n_col):
    pairs = []
    for m in range(n_row):
        takers = [(r, c) for c in range(m, n_col, n_row) for r in range(n_row)]
        cost = []
        for c in range(n_col):
            start = position(m, c, n_col)
            line = []
            for r, col in takers:
                far = sum(h * h + 4 * h for h in hops(start, position(r, col, n_col)))
                line.append(far + (100000 if r % 2 != c % 2 else 0))
            cost.append(line)
        for c, taker in enumerate(assign(cost)):
            r, col = takers[taker]
            pairs.append((m * n_col + c, r * n_col + col))
    return pairs


def copies_kernel(array, out):
    out[...] = jnp.broadcast_to(array[...][None], out.shape)


def spread(array, axes):
    copies = pl.pallas_call(
        copies_kernel,
        out_shape=jax.ShapeDtypeStruct((lax.axis_size(axes), *array.shape), array.dtype),
        in_specs=[vmem()],
        out_specs=vmem(),
        compiler_params=grant(2),
    )(array)
    return lax.all_to_all(copies, axes, 0, 0, tiled=True)


def shards(pairs, vectors, tiles, tile_rows, tile_cols, tile_count):
    axes = ("row", "col")
    n_row, n_col = lax.axis_size("row"), lax.axis_size("col")
    vecs, slots = vectors.shape[0], tiles.shape[0]
    pieces = n_col // 2
    row_index, col_index = lax.axis_index("row"), lax.axis_index("col")
    core, side = row_index % 2, col_index % 2
    swap = [(r, r ^ 1) for r in range(n_row)]

    col_place = ((tile_cols // n_col) ^ core) * n_col + tile_cols % n_col
    nothing = 2 * n_col
    live = jnp.arange(slots, dtype=jnp.int32) < tile_count[0]
    mirrored = live & ((row_index != col_index % n_row) | (tile_rows != tile_cols))
    mirror_source = jnp.where(mirrored, tile_rows, nothing)
    plain_source = jnp.where(live, col_place, nothing)

    own = spread(vectors, "col")
    mine = lax.dynamic_slice_in_dim(own, side * pieces, pieces, 0)
    mine = lax.ppermute(mine, axes, pairs)
    keep, give = products(True, tile_count, mirror_source, col_place, [own], tiles)
    came = lax.ppermute(give, "row", swap)
    sums = join(keep, came)
    sums = lax.ppermute(sums, axes, [(taker, giver) for giver, taker in pairs])

    theirs = lax.ppermute(mine, "row", swap)
    plain = products(False, tile_count, plain_source, tile_rows, [mine, theirs], tiles)
    plain = merge(side[None].astype(jnp.int32), plain, sums)
    plain = lax.all_to_all(plain, "col", 0, 0, tiled=True)
    return total(vecs, plain)


def solution(mesh):
    pairs = handing(mesh.shape["row"], mesh.shape["col"])

    def step(*args):
        return shards(pairs, *args)

    both = ("row", "col")
    return jax.shard_map(
        step,
        mesh=mesh,
        in_specs=(P(None, both), P(both, None, None), P(both), P(both), P(both)),
        out_specs=P(None, both),
        check_vma=False,
    )
```

```python
import functools

import jax
import jax.numpy as jnp
from jax import lax
from jax.experimental import pallas as pl
from jax.experimental.pallas import tpu as pltpu
from jax.sharding import PartitionSpec as P

CHUNK = 16
GROUP = 8
TOP = 14


def grant(mib):
    return pltpu.CompilerParams(vmem_limit_bytes=mib * 2**20)


def vmem():
    return pl.BlockSpec(memory_space=pltpu.VMEM)


def powers(exponent):
    low = exponent >> 1
    return (
        jnp.exp2(low.astype(jnp.float32)),
        jnp.exp2((exponent - low).astype(jnp.float32)),
    )


def pack(sums, payload, at):
    group, _, rows, width = sums.shape
    half = rows // 2
    peak = jnp.max(jnp.max(jnp.abs(sums), axis=1), axis=-1, keepdims=True)
    peak = jnp.maximum(peak, 1.2e-38)
    exponent = jnp.floor(jnp.log2(peak)).astype(jnp.int32)
    first, second = powers(TOP - exponent)
    for s in range(2):
        scaled = jnp.round((sums[:, s] * first) * second)
        scaled = jnp.minimum(jnp.maximum(scaled, -32767.0), 32767.0)
        scaled = scaled.astype(jnp.int32).astype(jnp.int16)
        payload[pl.ds(at, group), s * rows : (s + 1) * rows] = scaled
    lane = lax.broadcasted_iota(jnp.int32, (group, half, width), 2)
    both = jnp.where(lane < width // 2, exponent[:, :half], exponent[:, half:])
    payload[pl.ds(at, group), 2 * rows : 2 * rows + half] = both.astype(jnp.int16)


def unpack(payload, at, group, rows):
    half = rows // 2
    width = payload.shape[-1]
    exponent = payload[pl.ds(at, group), 2 * rows : 2 * rows + half].astype(jnp.int32)
    factors = []
    for factor in powers(exponent - TOP):
        upper = jnp.broadcast_to(factor[:, :, :1], (group, half, width))
        lower = factor[:, :, width // 2 : width // 2 + 1]
        lower = jnp.broadcast_to(lower, (group, half, width))
        factors.append(jnp.concatenate([upper, lower], axis=1))
    parts = [payload[pl.ds(at, group), s * rows : (s + 1) * rows] for s in range(2)]
    return [(part.astype(jnp.float32) * factors[0]) * factors[1] for part in parts]


def product_kernel(mirror, meta, sources, targets, *refs):
    if mirror:
        own, tiles, keep, give, x, held, sems, acc = refs
        parts = [own]
    else:
        mine, theirs, tiles, acc, x, held, sems = refs
        parts = [mine, theirs]
    width = tiles.shape[1]
    chunks = tiles.shape[0] // CHUNK

    def copy(step):
        part = pl.ds(step * CHUNK, CHUNK)
        return pltpu.make_async_copy(tiles.at[part], held.at[part], sems.at[step])

    for step in range(chunks):
        copy(step).start()
    at = 0
    for part in parts:
        size = part.shape[0]
        for s in range(2):
            x[at : at + size, s] = part[:, :, s * width : (s + 1) * width]
        at += size
    x[at] = jnp.zeros(x.shape[1:], x.dtype)
    acc[...] = jnp.zeros_like(acc)

    def step_body(step, carry):
        copy(step).wait()

        @pl.when(step * CHUNK < meta[0])
        def _():
            found = []
            for u in range(CHUNK):
                k = step * CHUNK + u
                source = sources[k]
                found.append(
                    lax.dot_general(
                        x[source // 2, source % 2],
                        held[k],
                        (((1,), (0 if mirror else 1,)), ((), ())),
                        preferred_element_type=jnp.float32,
                    )
                )
            for u in range(CHUNK):
                target = targets[step * CHUNK + u]
                acc[target // 2, target % 2] += found[u]

        return carry

    lax.fori_loop(0, chunks, step_body, 0)
    if mirror:
        half = keep.shape[0]
        keep[...] = acc[:half]
        give[...] = acc[half:]


def products(mirror, meta, sources, targets, segment, tiles):
    smem = pl.BlockSpec(memory_space=pltpu.SMEM)
    pieces = segment[0].shape[0] * len(segment)
    vecs = segment[0].shape[1]
    width = tiles.shape[1]
    scratch = [
        pltpu.VMEM((pieces + 1, 2, vecs, width), jnp.bfloat16),
        pltpu.VMEM(tiles.shape, tiles.dtype),
        pltpu.SemaphoreType.DMA((tiles.shape[0] // CHUNK,)),
    ]
    if mirror:
        shapes = [jax.ShapeDtypeStruct((pieces // 2, 2, vecs, width), jnp.float32)] * 2
        outs = [vmem(), vmem()]
        scratch.append(pltpu.VMEM((pieces, 2, vecs, width), jnp.float32))
    else:
        shapes = jax.ShapeDtypeStruct((pieces, 2, vecs, width), jnp.float32)
        outs = vmem()
    return pl.pallas_call(
        functools.partial(product_kernel, mirror),
        out_shape=shapes,
        in_specs=[smem] * 3 + [vmem()] * len(segment) + [pl.BlockSpec(memory_space=pltpu.HBM)],
        out_specs=outs,
        scratch_shapes=scratch,
        compiler_params=grant(12),
    )(meta, sources, targets, *segment, tiles)


def join_kernel(keep, came, payload):
    def body(i, carry):
        part = pl.ds(i * GROUP, GROUP)
        pack(keep[part] + came[part], payload, i * GROUP)
        return carry

    lax.fori_loop(0, payload.shape[0] // GROUP, body, 0)


def join(keep, came):
    pieces, _, vecs, width = keep.shape
    return pl.pallas_call(
        join_kernel,
        out_shape=jax.ShapeDtypeStruct((pieces, 5 * vecs // 2, width), jnp.int16),
        in_specs=[vmem()] * 2,
        out_specs=vmem(),
        compiler_params=grant(4),
    )(keep, came)


def merge_kernel(side, sums, came, payload):
    pieces, _, vecs, _ = sums.shape
    half = pieces // 2
    first, other = side[0] * half, (1 - side[0]) * half

    def body(i, carry):
        at = i * GROUP
        added = jnp.stack(unpack(came, at, GROUP, vecs), axis=1)
        pack(sums[pl.ds(first + at, GROUP)] + added, payload, first + at)
        pack(sums[pl.ds(other + at, GROUP)], payload, other + at)
        return carry

    lax.fori_loop(0, half // GROUP, body, 0)


def merge(side, sums, came):
    pieces, _, vecs, width = sums.shape
    return pl.pallas_call(
        merge_kernel,
        out_shape=jax.ShapeDtypeStruct((pieces, 5 * vecs // 2, width), jnp.int16),
        in_specs=[pl.BlockSpec(memory_space=pltpu.SMEM)] + [vmem()] * 2,
        out_specs=vmem(),
        compiler_params=grant(4),
    )(side, sums, came)


def total_kernel(vecs, payload, out):
    width = payload.shape[-1]

    def body(i, sums):
        parts = unpack(payload, i * GROUP, GROUP, vecs)
        return tuple(one + part.sum(axis=0) for one, part in zip(sums, parts))

    zero = jnp.zeros((vecs, width), jnp.float32)
    sums = lax.fori_loop(0, payload.shape[0] // GROUP, body, (zero, zero))
    for s in range(2):
        out[:, s * width : (s + 1) * width] = sums[s]


def total(vecs, payload):
    return pl.pallas_call(
        functools.partial(total_kernel, vecs),
        out_shape=jax.ShapeDtypeStruct((vecs, 2 * payload.shape[-1]), jnp.float32),
        in_specs=[vmem()],
        out_specs=vmem(),
        compiler_params=grant(4),
    )(payload)


def assign(cost):
    n = len(cost)
    row_price, col_price = [0] * (n + 1), [0] * (n + 1)
    owner, trail = [0] * (n + 1), [0] * (n + 1)
    for i in range(1, n + 1):
        owner[0], at = i, 0
        slack, seen = [float("inf")] * (n + 1), [False] * (n + 1)
        while owner[at]:
            seen[at] = True
            row, gap, nearest = owner[at], float("inf"), 0
            for c in range(1, n + 1):
                if not seen[c]:
                    left = cost[row - 1][c - 1] - row_price[row] - col_price[c]
                    if left < slack[c]:
                        slack[c], trail[c] = left, at
                    if slack[c] < gap:
                        gap, nearest = slack[c], c
            for c in range(n + 1):
                if seen[c]:
                    row_price[owner[c]] += gap
                    col_price[c] -= gap
                else:
                    slack[c] -= gap
            at = nearest
        while at:
            owner[at] = owner[trail[at]]
            at = trail[at]
    columns = [0] * n
    for c in range(1, n + 1):
        columns[owner[c] - 1] = c - 1
    return columns


def position(row, col, n_col):
    deep = n_col // 4
    return row // 4, (row // 2) % 2 * 4 + col // deep, col % deep


def hops(one, other, sides=(4, 8, 12)):
    return [min((p - q) % side, (q - p) % side) for p, q, side in zip(one, other, sides)]


def handing(n_row, n_col):
    pairs = []
    for m in range(n_row):
        takers = [(r, c) for c in range(m, n_col, n_row) for r in range(n_row)]
        cost = []
        for c in range(n_col):
            start = position(m, c, n_col)
            line = []
            for r, col in takers:
                far = sum(h * h + 4 * h for h in hops(start, position(r, col, n_col)))
                line.append(far + (100000 if r % 2 != c % 2 else 0))
            cost.append(line)
        for c, taker in enumerate(assign(cost)):
            r, col = takers[taker]
            pairs.append((m * n_col + c, r * n_col + col))
    return pairs


def copies_kernel(array, out):
    out[...] = jnp.broadcast_to(array[...][None], out.shape)


def spread(array, axes):
    copies = pl.pallas_call(
        copies_kernel,
        out_shape=pltpu.VMEM((lax.axis_size(axes), *array.shape), array.dtype),
        in_specs=[vmem()],
        out_specs=vmem(),
        compiler_params=grant(2),
    )(array)
    return lax.all_to_all(copies, axes, 0, 0, tiled=True)


def shards(pairs, vectors, tiles, tile_rows, tile_cols, tile_count):
    axes = ("row", "col")
    n_row, n_col = lax.axis_size("row"), lax.axis_size("col")
    vecs, slots = vectors.shape[0], tiles.shape[0]
    pieces = n_col // 2
    row_index, col_index = lax.axis_index("row"), lax.axis_index("col")
    core, side = row_index % 2, col_index % 2
    swap = [(r, r ^ 1) for r in range(n_row)]

    col_place = ((tile_cols // n_col) ^ core) * n_col + tile_cols % n_col
    nothing = 2 * n_col
    live = jnp.arange(slots, dtype=jnp.int32) < tile_count[0]
    mirrored = live & ((row_index != col_index % n_row) | (tile_rows != tile_cols))
    mirror_source = jnp.where(mirrored, tile_rows, nothing)
    plain_source = jnp.where(live, col_place, nothing)

    tiles = pltpu.with_memory_space_constraint(tiles, pltpu.HBM)
    own = spread(vectors, "col")
    mine = lax.dynamic_slice_in_dim(own, side * pieces, pieces, 0)
    mine = lax.ppermute(mine, axes, pairs)
    keep, give = products(True, tile_count, mirror_source, col_place, [own], tiles)
    came = lax.ppermute(give, "row", swap)
    sums = join(keep, came)
    sums = lax.ppermute(sums, axes, [(taker, giver) for giver, taker in pairs])

    theirs = lax.ppermute(mine, "row", swap)
    plain = products(False, tile_count, plain_source, tile_rows, [mine, theirs], tiles)
    plain = merge(side[None].astype(jnp.int32), plain, sums)
    plain = lax.all_to_all(plain, "col", 0, 0, tiled=True)
    return total(vecs, plain)


def solution(mesh):
    pairs = handing(mesh.shape["row"], mesh.shape["col"])

    def step(*args):
        return shards(pairs, *args)

    both = ("row", "col")
    return jax.shard_map(
        step,
        mesh=mesh,
        in_specs=(P(None, both), P(both, None, None), P(both), P(both), P(both)),
        out_specs=P(None, both),
        check_vma=False,
    )
```

```python
import functools

import jax
import jax.numpy as jnp
from jax import lax
from jax.experimental import pallas as pl
from jax.experimental.pallas import tpu as pltpu
from jax.sharding import PartitionSpec as P

CHUNK = 16
GROUP = 8
TOP = 14
TAKERS_OUT = (
    (8, 5, 4, 27, 20, 31, 34, 47, 46, 39, 38, 9, 12, 1, 24, 25, 28, 21, 16, 35, 44, 33, 0, 13, 6, 7, 18, 29, 30, 17, 32, 41, 40, 37, 36, 11, 10, 15, 14, 19, 22, 23, 26, 43, 42, 45, 2, 3),
    (8, 13, 0, 1, 16, 25, 30, 35, 38, 47, 42, 5, 4, 9, 12, 17, 24, 29, 28, 21, 36, 43, 34, 33, 2, 15, 6, 7, 20, 23, 26, 37, 44, 45, 40, 41, 14, 11, 10, 31, 18, 27, 22, 19, 32, 39, 46, 3),
    (6, 11, 10, 7, 2, 25, 28, 17, 40, 41, 44, 37, 32, 15, 14, 3, 22, 27, 26, 23, 30, 33, 36, 39, 34, 9, 0, 1, 18, 19, 24, 31, 46, 43, 42, 47, 12, 13, 8, 5, 4, 21, 20, 29, 16, 45, 38, 35),
    (44, 3, 10, 11, 6, 7, 18, 27, 20, 33, 40, 41, 42, 39, 2, 15, 14, 19, 30, 31, 26, 23, 34, 45, 38, 47, 4, 5, 8, 1, 16, 25, 22, 35, 46, 43, 32, 9, 0, 13, 12, 29, 28, 21, 24, 17, 36, 37),
    (46, 43, 8, 13, 12, 5, 4, 23, 18, 19, 42, 47, 34, 39, 38, 1, 0, 9, 16, 17, 28, 29, 24, 35, 40, 41, 44, 11, 10, 3, 20, 21, 22, 25, 36, 37, 32, 33, 6, 7, 14, 15, 2, 31, 30, 27, 26, 45),
    (38, 47, 46, 35, 12, 13, 8, 9, 26, 27, 30, 39, 42, 43, 34, 5, 4, 1, 0, 25, 24, 17, 28, 29, 44, 37, 36, 3, 6, 11, 2, 7, 16, 19, 20, 21, 40, 45, 32, 41, 10, 15, 14, 23, 22, 31, 18, 33),
    (36, 45, 44, 33, 32, 15, 14, 3, 10, 23, 26, 19, 22, 41, 40, 37, 6, 7, 2, 11, 18, 31, 30, 27, 34, 35, 46, 39, 38, 5, 8, 1, 4, 21, 16, 17, 24, 47, 42, 43, 0, 9, 12, 13, 20, 25, 28, 29),
    (24, 33, 32, 45, 44, 37, 10, 15, 2, 7, 16, 29, 30, 31, 36, 41, 40, 11, 6, 3, 14, 27, 18, 19, 26, 39, 38, 43, 46, 47, 4, 5, 0, 1, 22, 23, 20, 21, 34, 35, 42, 9, 8, 13, 12, 17, 28, 25),
    (18, 19, 26, 35, 38, 39, 34, 1, 0, 5, 4, 23, 22, 21, 42, 47, 46, 43, 12, 9, 8, 13, 24, 25, 16, 17, 20, 37, 44, 41, 40, 15, 14, 7, 28, 29, 30, 27, 36, 33, 32, 45, 6, 11, 2, 3, 10, 31),
    (26, 23, 18, 39, 34, 35, 46, 43, 0, 1, 12, 27, 28, 31, 24, 25, 42, 47, 38, 13, 4, 5, 8, 9, 20, 17, 16, 29, 32, 45, 36, 33, 10, 15, 6, 21, 22, 19, 30, 41, 40, 37, 44, 3, 2, 11, 14, 7),
    (16, 29, 24, 25, 20, 33, 40, 41, 44, 3, 6, 7, 10, 21, 22, 27, 36, 45, 32, 37, 14, 11, 2, 15, 30, 31, 18, 19, 26, 43, 38, 39, 46, 9, 8, 13, 4, 17, 28, 23, 42, 47, 34, 35, 12, 5, 0, 1),
    (2, 11, 20, 21, 24, 25, 32, 33, 40, 41, 14, 15, 6, 3, 28, 29, 30, 23, 44, 45, 36, 37, 10, 7, 12, 27, 22, 19, 18, 31, 46, 47, 42, 43, 8, 9, 0, 1, 26, 17, 16, 35, 38, 39, 34, 13, 4, 5),
    (14, 9, 30, 23, 26, 19, 42, 43, 46, 47, 38, 11, 0, 1, 12, 27, 22, 29, 20, 39, 34, 35, 4, 5, 8, 13, 28, 17, 24, 25, 16, 41, 32, 33, 44, 15, 10, 3, 2, 21, 18, 31, 40, 37, 36, 45, 6, 7),
    (12, 3, 6, 31, 18, 27, 22, 47, 38, 43, 34, 35, 8, 5, 4, 1, 30, 23, 26, 29, 42, 39, 46, 13, 0, 9, 10, 25, 16, 21, 20, 17, 44, 41, 32, 33, 2, 7, 14, 15, 24, 19, 28, 45, 40, 37, 36, 11),
    (40, 1, 0, 11, 28, 21, 20, 29, 32, 37, 36, 33, 6, 3, 2, 7, 10, 27, 24, 31, 30, 45, 44, 41, 14, 13, 8, 15, 26, 19, 22, 23, 18, 39, 38, 47, 42, 5, 4, 9, 12, 17, 16, 25, 46, 43, 34, 35),
    (36, 41, 10, 1, 0, 29, 20, 21, 28, 45, 32, 37, 44, 11, 6, 7, 2, 3, 30, 25, 16, 27, 40, 33, 38, 15, 14, 9, 4, 23, 18, 19, 22, 31, 46, 39, 34, 47, 12, 5, 8, 13, 26, 17, 24, 35, 42, 43),
)
TAKERS_BACK = (
    (8, 5, 4, 27, 20, 31, 34, 47, 46, 39, 38, 9, 12, 1, 24, 25, 28, 21, 16, 35, 44, 33, 0, 13, 6, 7, 18, 29, 30, 17, 32, 41, 40, 37, 36, 11, 10, 15, 14, 19, 22, 23, 26, 43, 42, 45, 2, 3),
    (8, 13, 0, 1, 16, 25, 30, 35, 38, 47, 42, 5, 4, 9, 12, 17, 24, 29, 28, 21, 36, 43, 34, 33, 2, 15, 6, 7, 20, 23, 26, 37, 44, 45, 40, 41, 14, 11, 10, 31, 18, 27, 22, 19, 32, 39, 46, 3),
    (6, 11, 10, 7, 2, 25, 28, 17, 40, 41, 44, 37, 32, 15, 14, 3, 22, 27, 26, 23, 30, 33, 36, 39, 34, 9, 0, 1, 18, 19, 24, 31, 46, 43, 42, 47, 12, 13, 8, 5, 4, 21, 20, 29, 16, 45, 38, 35),
    (44, 3, 10, 11, 6, 7, 18, 27, 20, 33, 40, 41, 42, 39, 2, 15, 14, 19, 30, 31, 26, 23, 34, 45, 38, 47, 4, 5, 8, 1, 16, 25, 22, 35, 46, 43, 32, 9, 0, 13, 12, 29, 28, 21, 24, 17, 36, 37),
    (46, 43, 8, 13, 12, 5, 4, 23, 18, 19, 42, 47, 34, 39, 38, 1, 0, 9, 16, 17, 28, 29, 24, 35, 40, 41, 44, 11, 10, 3, 20, 21, 22, 25, 36, 37, 32, 33, 6, 7, 14, 15, 2, 31, 30, 27, 26, 45),
    (38, 47, 46, 35, 12, 13, 8, 9, 26, 27, 30, 39, 42, 43, 34, 5, 4, 1, 0, 25, 24, 17, 28, 29, 44, 37, 36, 3, 6, 11, 2, 7, 16, 19, 20, 21, 40, 45, 32, 41, 10, 15, 14, 23, 22, 31, 18, 33),
    (36, 45, 44, 33, 32, 15, 14, 3, 10, 23, 26, 19, 22, 41, 40, 37, 6, 7, 2, 11, 18, 31, 30, 27, 34, 35, 46, 39, 38, 5, 8, 1, 4, 21, 16, 17, 24, 47, 42, 43, 0, 9, 12, 13, 20, 25, 28, 29),
    (24, 33, 32, 45, 44, 37, 10, 15, 2, 7, 16, 29, 30, 31, 36, 41, 40, 11, 6, 3, 14, 27, 18, 19, 26, 39, 38, 43, 46, 47, 4, 5, 0, 1, 22, 23, 20, 21, 34, 35, 42, 9, 8, 13, 12, 17, 28, 25),
    (18, 19, 26, 35, 38, 39, 34, 1, 0, 5, 4, 23, 22, 21, 42, 47, 46, 43, 12, 9, 8, 13, 24, 25, 16, 17, 20, 37, 44, 41, 40, 15, 14, 7, 28, 29, 30, 27, 36, 33, 32, 45, 6, 11, 2, 3, 10, 31),
    (26, 23, 18, 39, 34, 35, 46, 43, 0, 1, 12, 27, 28, 31, 24, 25, 42, 47, 38, 13, 4, 5, 8, 9, 20, 17, 16, 29, 32, 45, 36, 33, 10, 15, 6, 21, 22, 19, 30, 41, 40, 37, 44, 3, 2, 11, 14, 7),
    (16, 29, 24, 25, 20, 33, 40, 41, 44, 3, 6, 7, 10, 21, 22, 27, 36, 45, 32, 37, 14, 11, 2, 15, 30, 31, 18, 19, 26, 43, 38, 39, 46, 9, 8, 13, 4, 17, 28, 23, 42, 47, 34, 35, 12, 5, 0, 1),
    (2, 11, 20, 21, 24, 25, 32, 33, 40, 41, 14, 15, 6, 3, 28, 29, 30, 23, 44, 45, 36, 37, 10, 7, 12, 27, 22, 19, 18, 31, 46, 47, 42, 43, 8, 9, 0, 1, 26, 17, 16, 35, 38, 39, 34, 13, 4, 5),
    (14, 9, 30, 23, 26, 19, 42, 43, 46, 47, 38, 11, 0, 1, 12, 27, 22, 29, 20, 39, 34, 35, 4, 5, 8, 13, 28, 17, 24, 25, 16, 41, 32, 33, 44, 15, 10, 3, 2, 21, 18, 31, 40, 37, 36, 45, 6, 7),
    (12, 3, 6, 31, 18, 27, 22, 47, 38, 43, 34, 35, 8, 5, 4, 1, 30, 23, 26, 29, 42, 39, 46, 13, 0, 9, 10, 25, 16, 21, 20, 17, 44, 41, 32, 33, 2, 7, 14, 15, 24, 19, 28, 45, 40, 37, 36, 11),
    (40, 1, 0, 11, 28, 21, 20, 29, 32, 37, 36, 33, 6, 3, 2, 7, 10, 27, 24, 31, 30, 45, 44, 41, 14, 13, 8, 15, 26, 19, 22, 23, 18, 39, 38, 47, 42, 5, 4, 9, 12, 17, 16, 25, 46, 43, 34, 35),
    (36, 41, 10, 1, 0, 29, 20, 21, 28, 45, 32, 37, 44, 11, 6, 7, 2, 3, 30, 25, 16, 27, 40, 33, 38, 15, 14, 9, 4, 23, 18, 19, 22, 31, 46, 39, 34, 47, 12, 5, 8, 13, 26, 17, 24, 35, 42, 43),
)


def grant(mib):
    return pltpu.CompilerParams(vmem_limit_bytes=mib * 2**20)


def vmem():
    return pl.BlockSpec(memory_space=pltpu.VMEM)


def powers(exponent):
    low = exponent >> 1
    return (
        jnp.exp2(low.astype(jnp.float32)),
        jnp.exp2((exponent - low).astype(jnp.float32)),
    )


def pack(sums, payload, at):
    group, _, rows, width = sums.shape
    half = rows // 2
    peak = jnp.max(jnp.max(jnp.abs(sums), axis=1), axis=-1, keepdims=True)
    peak = jnp.maximum(peak, 1.2e-38)
    exponent = jnp.floor(jnp.log2(peak)).astype(jnp.int32)
    first, second = powers(TOP - exponent)
    for s in range(2):
        scaled = jnp.round((sums[:, s] * first) * second)
        scaled = jnp.minimum(jnp.maximum(scaled, -32767.0), 32767.0)
        scaled = scaled.astype(jnp.int32).astype(jnp.int16)
        payload[pl.ds(at, group), s * rows : (s + 1) * rows] = scaled
    lane = lax.broadcasted_iota(jnp.int32, (group, half, width), 2)
    both = jnp.where(lane < width // 2, exponent[:, :half], exponent[:, half:])
    payload[pl.ds(at, group), 2 * rows : 2 * rows + half] = both.astype(jnp.int16)


def unpack(payload, at, group, rows):
    half = rows // 2
    width = payload.shape[-1]
    exponent = payload[pl.ds(at, group), 2 * rows : 2 * rows + half].astype(jnp.int32)
    factors = []
    for factor in powers(exponent - TOP):
        upper = jnp.broadcast_to(factor[:, :, :1], (group, half, width))
        lower = factor[:, :, width // 2 : width // 2 + 1]
        lower = jnp.broadcast_to(lower, (group, half, width))
        factors.append(jnp.concatenate([upper, lower], axis=1))
    parts = [payload[pl.ds(at, group), s * rows : (s + 1) * rows] for s in range(2)]
    return [(part.astype(jnp.float32) * factors[0]) * factors[1] for part in parts]


def product_kernel(mirror, meta, sources, targets, *refs):
    if mirror:
        own, tiles, keep, give, x, held, sems, acc = refs
        parts = [own]
    else:
        mine, theirs, held, acc, x = refs
        parts = [mine, theirs]
    width = held.shape[1]
    chunks = held.shape[0] // CHUNK

    def copy(step):
        part = pl.ds(step * CHUNK, CHUNK)
        return pltpu.make_async_copy(tiles.at[part], held.at[part], sems.at[step])

    if mirror:
        for step in range(chunks):
            copy(step).start()
    at = 0
    for part in parts:
        size = part.shape[0]
        for s in range(2):
            x[at : at + size, s] = part[:, :, s * width : (s + 1) * width]
        at += size
    x[at] = jnp.zeros(x.shape[1:], x.dtype)
    acc[...] = jnp.zeros_like(acc)

    def step_body(step, carry):
        if mirror:
            copy(step).wait()

        @pl.when(step * CHUNK < meta[0])
        def _():
            found = []
            for u in range(CHUNK):
                k = step * CHUNK + u
                source = sources[k]
                found.append(
                    lax.dot_general(
                        x[source // 2, source % 2],
                        held[k],
                        (((1,), (0 if mirror else 1,)), ((), ())),
                        preferred_element_type=jnp.float32,
                    )
                )
            for u in range(CHUNK):
                target = targets[step * CHUNK + u]
                acc[target // 2, target % 2] += found[u]

        return carry

    lax.fori_loop(0, chunks, step_body, 0)
    if mirror:
        half = keep.shape[0]
        keep[...] = acc[:half]
        give[...] = acc[half:]


def products(mirror, meta, sources, targets, segment, tiles):
    smem = pl.BlockSpec(memory_space=pltpu.SMEM)
    space = pltpu.HBM if mirror else pltpu.VMEM
    tiles = pltpu.with_memory_space_constraint(tiles, space)
    pieces = segment[0].shape[0] * len(segment)
    vecs = segment[0].shape[1]
    width = tiles.shape[1]
    scratch = [pltpu.VMEM((pieces + 1, 2, vecs, width), jnp.bfloat16)]
    if mirror:
        shapes = [jax.ShapeDtypeStruct((pieces // 2, 2, vecs, width), jnp.float32)] * 2
        outs = [vmem(), vmem()]
        scratch += [
            pltpu.VMEM(tiles.shape, tiles.dtype),
            pltpu.SemaphoreType.DMA((tiles.shape[0] // CHUNK,)),
            pltpu.VMEM((pieces, 2, vecs, width), jnp.float32),
        ]
    else:
        shapes = jax.ShapeDtypeStruct((pieces, 2, vecs, width), jnp.float32)
        outs = vmem()
    return pl.pallas_call(
        functools.partial(product_kernel, mirror),
        out_shape=shapes,
        in_specs=[smem] * 3 + [vmem()] * len(segment) + [pl.BlockSpec(memory_space=space)],
        out_specs=outs,
        scratch_shapes=scratch,
        compiler_params=grant(12 if mirror else 4),
    )(meta, sources, targets, *segment, tiles)


def join_kernel(keep, came, payload):
    def body(i, carry):
        part = pl.ds(i * GROUP, GROUP)
        pack(keep[part] + came[part], payload, i * GROUP)
        return carry

    lax.fori_loop(0, payload.shape[0] // GROUP, body, 0)


def join(keep, came):
    pieces, _, vecs, width = keep.shape
    return pl.pallas_call(
        join_kernel,
        out_shape=jax.ShapeDtypeStruct((pieces, 5 * vecs // 2, width), jnp.int16),
        in_specs=[vmem()] * 2,
        out_specs=vmem(),
        compiler_params=grant(4),
    )(keep, came)


def merge_kernel(side, sums, came, payload):
    pieces, _, vecs, _ = sums.shape
    half = pieces // 2
    first, other = side[0] * half, (1 - side[0]) * half

    def body(i, carry):
        at = i * GROUP
        added = jnp.stack(unpack(came, at, GROUP, vecs), axis=1)
        pack(sums[pl.ds(first + at, GROUP)] + added, payload, first + at)
        pack(sums[pl.ds(other + at, GROUP)], payload, other + at)
        return carry

    lax.fori_loop(0, half // GROUP, body, 0)


def merge(side, sums, came):
    pieces, _, vecs, width = sums.shape
    return pl.pallas_call(
        merge_kernel,
        out_shape=jax.ShapeDtypeStruct((pieces, 5 * vecs // 2, width), jnp.int16),
        in_specs=[pl.BlockSpec(memory_space=pltpu.SMEM)] + [vmem()] * 2,
        out_specs=vmem(),
        compiler_params=grant(4),
    )(side, sums, came)


def total_kernel(vecs, payload, out):
    width = payload.shape[-1]

    def body(i, sums):
        parts = unpack(payload, i * GROUP, GROUP, vecs)
        return tuple(one + part.sum(axis=0) for one, part in zip(sums, parts))

    zero = jnp.zeros((vecs, width), jnp.float32)
    sums = lax.fori_loop(0, payload.shape[0] // GROUP, body, (zero, zero))
    for s in range(2):
        out[:, s * width : (s + 1) * width] = sums[s]


def total(vecs, payload):
    return pl.pallas_call(
        functools.partial(total_kernel, vecs),
        out_shape=jax.ShapeDtypeStruct((vecs, 2 * payload.shape[-1]), jnp.float32),
        in_specs=[vmem()],
        out_specs=vmem(),
        compiler_params=grant(4),
    )(payload)


def handing(table, n_row, n_col):
    pairs = []
    for m in range(n_row):
        takers = [(r, c) for c in range(m, n_col, n_row) for r in range(n_row)]
        for c, taker in enumerate(table[m]):
            r, col = takers[taker]
            pairs.append((m * n_col + c, r * n_col + col))
    return pairs


def copies_kernel(array, out, sems):
    copies = [
        pltpu.make_async_copy(array, out.at[i], sems.at[i]) for i in range(out.shape[0])
    ]
    for copy in copies:
        copy.start()
    for copy in copies:
        copy.wait()


def spread(array, axes):
    size = lax.axis_size(axes)
    hbm = pl.BlockSpec(memory_space=pltpu.HBM)
    copies = pl.pallas_call(
        copies_kernel,
        out_shape=jax.ShapeDtypeStruct((size, *array.shape), array.dtype),
        in_specs=[hbm],
        out_specs=hbm,
        scratch_shapes=[pltpu.SemaphoreType.DMA((size,))],
        compiler_params=grant(2),
    )(pltpu.with_memory_space_constraint(array, pltpu.HBM))
    return lax.all_to_all(copies, axes, 0, 0, tiled=True)


def shards(out, back, vectors, tiles, tile_rows, tile_cols, tile_count):
    axes = ("row", "col")
    n_row, n_col = lax.axis_size("row"), lax.axis_size("col")
    vecs, slots = vectors.shape[0], tiles.shape[0]
    pieces = n_col // 2
    row_index, col_index = lax.axis_index("row"), lax.axis_index("col")
    core, side = row_index % 2, col_index % 2
    swap = [(r, r ^ 1) for r in range(n_row)]

    col_place = ((tile_cols // n_col) ^ core) * n_col + tile_cols % n_col
    nothing = 2 * n_col
    live = jnp.arange(slots, dtype=jnp.int32) < tile_count[0]
    mirrored = live & ((row_index != col_index % n_row) | (tile_rows != tile_cols))
    mirror_source = jnp.where(mirrored, tile_rows, nothing)
    plain_source = jnp.where(live, col_place, nothing)

    own = spread(vectors, "col")
    mine = lax.dynamic_slice_in_dim(own, side * pieces, pieces, 0)
    mine = lax.ppermute(mine, axes, out)
    keep, give = products(True, tile_count, mirror_source, col_place, [own], tiles)
    came = lax.ppermute(give, "row", swap)
    sums = join(keep, came)
    sums = lax.ppermute(sums, axes, back)

    theirs = lax.ppermute(mine, "row", swap)
    plain = products(False, tile_count, plain_source, tile_rows, [mine, theirs], tiles)
    plain = merge(side[None].astype(jnp.int32), plain, sums)
    plain = lax.all_to_all(plain, "col", 0, 0, tiled=True)
    return total(vecs, plain)


def solution(mesh):
    sizes = mesh.shape["row"], mesh.shape["col"]
    out = handing(TAKERS_OUT, *sizes)
    back = [(taker, giver) for giver, taker in handing(TAKERS_BACK, *sizes)]

    def step(*args):
        return shards(out, back, *args)

    both = ("row", "col")
    return jax.shard_map(
        step,
        mesh=mesh,
        in_specs=(P(None, both), P(both, None, None), P(both), P(both), P(both)),
        out_specs=P(None, both),
        check_vma=False,
    )
```

```python
import functools

import jax
import jax.numpy as jnp
from jax import lax
from jax.experimental import pallas as pl
from jax.experimental.pallas import tpu as pltpu
from jax.sharding import PartitionSpec as P

CHUNK = 16
GROUP = 8
TOP = 14
TAKERS_OUT = (
    (8, 5, 4, 27, 20, 31, 34, 47, 46, 39, 38, 9, 12, 1, 24, 25, 28, 21, 16, 35, 44, 33, 0, 13, 6, 7, 18, 29, 30, 17, 32, 41, 40, 37, 36, 11, 10, 15, 14, 19, 22, 23, 26, 43, 42, 45, 2, 3),
    (8, 13, 0, 1, 16, 25, 30, 35, 38, 47, 42, 5, 4, 9, 12, 17, 24, 29, 28, 21, 36, 43, 34, 33, 2, 15, 6, 7, 20, 23, 26, 37, 44, 45, 40, 41, 14, 11, 10, 31, 18, 27, 22, 19, 32, 39, 46, 3),
    (6, 11, 10, 7, 2, 25, 28, 17, 40, 41, 44, 37, 32, 15, 14, 3, 22, 27, 26, 23, 30, 33, 36, 39, 34, 9, 0, 1, 18, 19, 24, 31, 46, 43, 42, 47, 12, 13, 8, 5, 4, 21, 20, 29, 16, 45, 38, 35),
    (44, 3, 10, 11, 6, 7, 18, 27, 20, 33, 40, 41, 42, 39, 2, 15, 14, 19, 30, 31, 26, 23, 34, 45, 38, 47, 4, 5, 8, 1, 16, 25, 22, 35, 46, 43, 32, 9, 0, 13, 12, 29, 28, 21, 24, 17, 36, 37),
    (46, 43, 8, 13, 12, 5, 4, 23, 18, 19, 42, 47, 34, 39, 38, 1, 0, 9, 16, 17, 28, 29, 24, 35, 40, 41, 44, 11, 10, 3, 20, 21, 22, 25, 36, 37, 32, 33, 6, 7, 14, 15, 2, 31, 30, 27, 26, 45),
    (38, 47, 46, 35, 12, 13, 8, 9, 26, 27, 30, 39, 42, 43, 34, 5, 4, 1, 0, 25, 24, 17, 28, 29, 44, 37, 36, 3, 6, 11, 2, 7, 16, 19, 20, 21, 40, 45, 32, 41, 10, 15, 14, 23, 22, 31, 18, 33),
    (36, 45, 44, 33, 32, 15, 14, 3, 10, 23, 26, 19, 22, 41, 40, 37, 6, 7, 2, 11, 18, 31, 30, 27, 34, 35, 46, 39, 38, 5, 8, 1, 4, 21, 16, 17, 24, 47, 42, 43, 0, 9, 12, 13, 20, 25, 28, 29),
    (24, 33, 32, 45, 44, 37, 10, 15, 2, 7, 16, 29, 30, 31, 36, 41, 40, 11, 6, 3, 14, 27, 18, 19, 26, 39, 38, 43, 46, 47, 4, 5, 0, 1, 22, 23, 20, 21, 34, 35, 42, 9, 8, 13, 12, 17, 28, 25),
    (18, 19, 26, 35, 38, 39, 34, 1, 0, 5, 4, 23, 22, 21, 42, 47, 46, 43, 12, 9, 8, 13, 24, 25, 16, 17, 20, 37, 44, 41, 40, 15, 14, 7, 28, 29, 30, 27, 36, 33, 32, 45, 6, 11, 2, 3, 10, 31),
    (26, 23, 18, 39, 34, 35, 46, 43, 0, 1, 12, 27, 28, 31, 24, 25, 42, 47, 38, 13, 4, 5, 8, 9, 20, 17, 16, 29, 32, 45, 36, 33, 10, 15, 6, 21, 22, 19, 30, 41, 40, 37, 44, 3, 2, 11, 14, 7),
    (16, 29, 24, 25, 20, 33, 40, 41, 44, 3, 6, 7, 10, 21, 22, 27, 36, 45, 32, 37, 14, 11, 2, 15, 30, 31, 18, 19, 26, 43, 38, 39, 46, 9, 8, 13, 4, 17, 28, 23, 42, 47, 34, 35, 12, 5, 0, 1),
    (2, 11, 20, 21, 24, 25, 32, 33, 40, 41, 14, 15, 6, 3, 28, 29, 30, 23, 44, 45, 36, 37, 10, 7, 12, 27, 22, 19, 18, 31, 46, 47, 42, 43, 8, 9, 0, 1, 26, 17, 16, 35, 38, 39, 34, 13, 4, 5),
    (14, 9, 30, 23, 26, 19, 42, 43, 46, 47, 38, 11, 0, 1, 12, 27, 22, 29, 20, 39, 34, 35, 4, 5, 8, 13, 28, 17, 24, 25, 16, 41, 32, 33, 44, 15, 10, 3, 2, 21, 18, 31, 40, 37, 36, 45, 6, 7),
    (12, 3, 6, 31, 18, 27, 22, 47, 38, 43, 34, 35, 8, 5, 4, 1, 30, 23, 26, 29, 42, 39, 46, 13, 0, 9, 10, 25, 16, 21, 20, 17, 44, 41, 32, 33, 2, 7, 14, 15, 24, 19, 28, 45, 40, 37, 36, 11),
    (40, 1, 0, 11, 28, 21, 20, 29, 32, 37, 36, 33, 6, 3, 2, 7, 10, 27, 24, 31, 30, 45, 44, 41, 14, 13, 8, 15, 26, 19, 22, 23, 18, 39, 38, 47, 42, 5, 4, 9, 12, 17, 16, 25, 46, 43, 34, 35),
    (36, 41, 10, 1, 0, 29, 20, 21, 28, 45, 32, 37, 44, 11, 6, 7, 2, 3, 30, 25, 16, 27, 40, 33, 38, 15, 14, 9, 4, 23, 18, 19, 22, 31, 46, 39, 34, 47, 12, 5, 8, 13, 26, 17, 24, 35, 42, 43),
)
TAKERS_BACK = (
    (8, 5, 4, 27, 20, 31, 34, 47, 46, 39, 38, 9, 12, 1, 24, 25, 28, 21, 16, 35, 44, 33, 0, 13, 6, 7, 18, 29, 30, 17, 32, 41, 40, 37, 36, 11, 10, 15, 14, 19, 22, 23, 26, 43, 42, 45, 2, 3),
    (8, 13, 0, 1, 16, 25, 30, 35, 38, 47, 42, 5, 4, 9, 12, 17, 24, 29, 28, 21, 36, 43, 34, 33, 2, 15, 6, 7, 20, 23, 26, 37, 44, 45, 40, 41, 14, 11, 10, 31, 18, 27, 22, 19, 32, 39, 46, 3),
    (6, 11, 10, 7, 2, 25, 28, 17, 40, 41, 44, 37, 32, 15, 14, 3, 22, 27, 26, 23, 30, 33, 36, 39, 34, 9, 0, 1, 18, 19, 24, 31, 46, 43, 42, 47, 12, 13, 8, 5, 4, 21, 20, 29, 16, 45, 38, 35),
    (44, 3, 10, 11, 6, 7, 18, 27, 20, 33, 40, 41, 42, 39, 2, 15, 14, 19, 30, 31, 26, 23, 34, 45, 38, 47, 4, 5, 8, 1, 16, 25, 22, 35, 46, 43, 32, 9, 0, 13, 12, 29, 28, 21, 24, 17, 36, 37),
    (46, 43, 8, 13, 12, 5, 4, 23, 18, 19, 42, 47, 34, 39, 38, 1, 0, 9, 16, 17, 28, 29, 24, 35, 40, 41, 44, 11, 10, 3, 20, 21, 22, 25, 36, 37, 32, 33, 6, 7, 14, 15, 2, 31, 30, 27, 26, 45),
    (38, 47, 46, 35, 12, 13, 8, 9, 26, 27, 30, 39, 42, 43, 34, 5, 4, 1, 0, 25, 24, 17, 28, 29, 44, 37, 36, 3, 6, 11, 2, 7, 16, 19, 20, 21, 40, 45, 32, 41, 10, 15, 14, 23, 22, 31, 18, 33),
    (36, 45, 44, 33, 32, 15, 14, 3, 10, 23, 26, 19, 22, 41, 40, 37, 6, 7, 2, 11, 18, 31, 30, 27, 34, 35, 46, 39, 38, 5, 8, 1, 4, 21, 16, 17, 24, 47, 42, 43, 0, 9, 12, 13, 20, 25, 28, 29),
    (24, 33, 32, 45, 44, 37, 10, 15, 2, 7, 16, 29, 30, 31, 36, 41, 40, 11, 6, 3, 14, 27, 18, 19, 26, 39, 38, 43, 46, 47, 4, 5, 0, 1, 22, 23, 20, 21, 34, 35, 42, 9, 8, 13, 12, 17, 28, 25),
    (18, 19, 26, 35, 38, 39, 34, 1, 0, 5, 4, 23, 22, 21, 42, 47, 46, 43, 12, 9, 8, 13, 24, 25, 16, 17, 20, 37, 44, 41, 40, 15, 14, 7, 28, 29, 30, 27, 36, 33, 32, 45, 6, 11, 2, 3, 10, 31),
    (26, 23, 18, 39, 34, 35, 46, 43, 0, 1, 12, 27, 28, 31, 24, 25, 42, 47, 38, 13, 4, 5, 8, 9, 20, 17, 16, 29, 32, 45, 36, 33, 10, 15, 6, 21, 22, 19, 30, 41, 40, 37, 44, 3, 2, 11, 14, 7),
    (16, 29, 24, 25, 20, 33, 40, 41, 44, 3, 6, 7, 10, 21, 22, 27, 36, 45, 32, 37, 14, 11, 2, 15, 30, 31, 18, 19, 26, 43, 38, 39, 46, 9, 8, 13, 4, 17, 28, 23, 42, 47, 34, 35, 12, 5, 0, 1),
    (2, 11, 20, 21, 24, 25, 32, 33, 40, 41, 14, 15, 6, 3, 28, 29, 30, 23, 44, 45, 36, 37, 10, 7, 12, 27, 22, 19, 18, 31, 46, 47, 42, 43, 8, 9, 0, 1, 26, 17, 16, 35, 38, 39, 34, 13, 4, 5),
    (14, 9, 30, 23, 26, 19, 42, 43, 46, 47, 38, 11, 0, 1, 12, 27, 22, 29, 20, 39, 34, 35, 4, 5, 8, 13, 28, 17, 24, 25, 16, 41, 32, 33, 44, 15, 10, 3, 2, 21, 18, 31, 40, 37, 36, 45, 6, 7),
    (12, 3, 6, 31, 18, 27, 22, 47, 38, 43, 34, 35, 8, 5, 4, 1, 30, 23, 26, 29, 42, 39, 46, 13, 0, 9, 10, 25, 16, 21, 20, 17, 44, 41, 32, 33, 2, 7, 14, 15, 24, 19, 28, 45, 40, 37, 36, 11),
    (40, 1, 0, 11, 28, 21, 20, 29, 32, 37, 36, 33, 6, 3, 2, 7, 10, 27, 24, 31, 30, 45, 44, 41, 14, 13, 8, 15, 26, 19, 22, 23, 18, 39, 38, 47, 42, 5, 4, 9, 12, 17, 16, 25, 46, 43, 34, 35),
    (36, 41, 10, 1, 0, 29, 20, 21, 28, 45, 32, 37, 44, 11, 6, 7, 2, 3, 30, 25, 16, 27, 40, 33, 38, 15, 14, 9, 4, 23, 18, 19, 22, 31, 46, 39, 34, 47, 12, 5, 8, 13, 26, 17, 24, 35, 42, 43),
)


def grant(mib):
    return pltpu.CompilerParams(vmem_limit_bytes=mib * 2**20)


def vmem():
    return pl.BlockSpec(memory_space=pltpu.VMEM)


def powers(exponent):
    low = exponent >> 1
    return (
        jnp.exp2(low.astype(jnp.float32)),
        jnp.exp2((exponent - low).astype(jnp.float32)),
    )


def pack(sums, payload, at):
    group, _, rows, width = sums.shape
    half = rows // 2
    peak = jnp.max(jnp.max(jnp.abs(sums), axis=1), axis=-1, keepdims=True)
    peak = jnp.maximum(peak, 1.2e-38)
    exponent = jnp.floor(jnp.log2(peak)).astype(jnp.int32)
    first, second = powers(TOP - exponent)
    for s in range(2):
        scaled = jnp.round((sums[:, s] * first) * second)
        scaled = jnp.minimum(jnp.maximum(scaled, -32767.0), 32767.0)
        scaled = scaled.astype(jnp.int32).astype(jnp.int16)
        payload[pl.ds(at, group), s * rows : (s + 1) * rows] = scaled
    lane = lax.broadcasted_iota(jnp.int32, (group, half, width), 2)
    both = jnp.where(lane < width // 2, exponent[:, :half], exponent[:, half:])
    payload[pl.ds(at, group), 2 * rows : 2 * rows + half] = both.astype(jnp.int16)


def unpack(payload, at, group, rows):
    half = rows // 2
    width = payload.shape[-1]
    exponent = payload[pl.ds(at, group), 2 * rows : 2 * rows + half].astype(jnp.int32)
    factors = []
    for factor in powers(exponent - TOP):
        upper = jnp.broadcast_to(factor[:, :, :1], (group, half, width))
        lower = factor[:, :, width // 2 : width // 2 + 1]
        lower = jnp.broadcast_to(lower, (group, half, width))
        factors.append(jnp.concatenate([upper, lower], axis=1))
    parts = [payload[pl.ds(at, group), s * rows : (s + 1) * rows] for s in range(2)]
    return [(part.astype(jnp.float32) * factors[0]) * factors[1] for part in parts]


def product_kernel(mirror, meta, sources, targets, *refs):
    if mirror:
        own, tiles, keep, give, x, held, sems, acc = refs
        parts = [own]
    else:
        mine, theirs, held, acc, x = refs
        parts = [mine, theirs]
    width = held.shape[1]
    chunks = held.shape[0] // CHUNK

    def copy(step):
        part = pl.ds(step * CHUNK, CHUNK)
        return pltpu.make_async_copy(tiles.at[part], held.at[part], sems.at[step])

    if mirror:
        for step in range(chunks):
            copy(step).start()
    at = 0
    for part in parts:
        size = part.shape[0]
        for s in range(2):
            x[at : at + size, s] = part[:, :, s * width : (s + 1) * width]
        at += size
    x[at] = jnp.zeros(x.shape[1:], x.dtype)
    acc[...] = jnp.zeros_like(acc)

    def step_body(step, carry):
        if mirror:
            copy(step).wait()

        @pl.when(step * CHUNK < meta[0])
        def _():
            found = []
            for u in range(CHUNK):
                k = step * CHUNK + u
                source = sources[k]
                found.append(
                    lax.dot_general(
                        x[source // 2, source % 2],
                        held[k],
                        (((1,), (0 if mirror else 1,)), ((), ())),
                        preferred_element_type=jnp.float32,
                    )
                )
            for u in range(CHUNK):
                target = targets[step * CHUNK + u]
                acc[target // 2, target % 2] += found[u]

        return carry

    lax.fori_loop(0, chunks, step_body, 0)
    if mirror:
        half = keep.shape[0]
        keep[...] = acc[:half]
        give[...] = acc[half:]


def products(mirror, meta, sources, targets, segment, tiles):
    smem = pl.BlockSpec(memory_space=pltpu.SMEM)
    space = pltpu.HBM if mirror else pltpu.VMEM
    tiles = pltpu.with_memory_space_constraint(tiles, space)
    pieces = segment[0].shape[0] * len(segment)
    vecs = segment[0].shape[1]
    width = tiles.shape[1]
    scratch = [pltpu.VMEM((pieces + 1, 2, vecs, width), jnp.bfloat16)]
    if mirror:
        shapes = [jax.ShapeDtypeStruct((pieces // 2, 2, vecs, width), jnp.float32)] * 2
        outs = [vmem(), vmem()]
        scratch += [
            pltpu.VMEM(tiles.shape, tiles.dtype),
            pltpu.SemaphoreType.DMA((tiles.shape[0] // CHUNK,)),
            pltpu.VMEM((pieces, 2, vecs, width), jnp.float32),
        ]
    else:
        shapes = jax.ShapeDtypeStruct((pieces, 2, vecs, width), jnp.float32)
        outs = vmem()
    return pl.pallas_call(
        functools.partial(product_kernel, mirror),
        out_shape=shapes,
        in_specs=[smem] * 3 + [vmem()] * len(segment) + [pl.BlockSpec(memory_space=space)],
        out_specs=outs,
        scratch_shapes=scratch,
        compiler_params=grant(12 if mirror else 4),
    )(meta, sources, targets, *segment, tiles)


def join_kernel(keep, came, payload):
    def body(i, carry):
        part = pl.ds(i * GROUP, GROUP)
        pack(keep[part] + came[part], payload, i * GROUP)
        return carry

    lax.fori_loop(0, payload.shape[0] // GROUP, body, 0)


def join(keep, came):
    pieces, _, vecs, width = keep.shape
    return pl.pallas_call(
        join_kernel,
        out_shape=jax.ShapeDtypeStruct((pieces, 5 * vecs // 2, width), jnp.int16),
        in_specs=[vmem()] * 2,
        out_specs=vmem(),
        compiler_params=grant(4),
    )(keep, came)


def merge_kernel(side, sums, came, payload):
    pieces, _, vecs, _ = sums.shape
    half = pieces // 2
    first, other = side[0] * half, (1 - side[0]) * half

    def body(i, carry):
        at = i * GROUP
        added = jnp.stack(unpack(came, at, GROUP, vecs), axis=1)
        pack(sums[pl.ds(first + at, GROUP)] + added, payload, first + at)
        pack(sums[pl.ds(other + at, GROUP)], payload, other + at)
        return carry

    lax.fori_loop(0, half // GROUP, body, 0)


def merge(side, sums, came):
    pieces, _, vecs, width = sums.shape
    return pl.pallas_call(
        merge_kernel,
        out_shape=jax.ShapeDtypeStruct((pieces, 5 * vecs // 2, width), jnp.int16),
        in_specs=[pl.BlockSpec(memory_space=pltpu.SMEM)] + [vmem()] * 2,
        out_specs=vmem(),
        compiler_params=grant(4),
    )(side, sums, came)


def total_kernel(vecs, payload, out):
    width = payload.shape[-1]

    def body(i, sums):
        parts = unpack(payload, i * GROUP, GROUP, vecs)
        return tuple(one + part.sum(axis=0) for one, part in zip(sums, parts))

    zero = jnp.zeros((vecs, width), jnp.float32)
    sums = lax.fori_loop(0, payload.shape[0] // GROUP, body, (zero, zero))
    for s in range(2):
        out[:, s * width : (s + 1) * width] = sums[s]


def total(vecs, payload):
    return pl.pallas_call(
        functools.partial(total_kernel, vecs),
        out_shape=jax.ShapeDtypeStruct((vecs, 2 * payload.shape[-1]), jnp.float32),
        in_specs=[vmem()],
        out_specs=vmem(),
        compiler_params=grant(4),
    )(payload)


def handing(table, n_row, n_col):
    pairs = []
    for m in range(n_row):
        takers = [(r, c) for c in range(m, n_col, n_row) for r in range(n_row)]
        for c, taker in enumerate(table[m]):
            r, col = takers[taker]
            pairs.append((m * n_col + c, r * n_col + col))
    return pairs


def copies_kernel(array, out, held, sem):
    copy = pltpu.make_async_copy(array, held, sem)
    copy.start()
    copy.wait()
    out[...] = jnp.broadcast_to(held[...][None], out.shape)


def spread(array, axes):
    size = lax.axis_size(axes)
    return lax.all_to_all(
        pl.pallas_call(
            copies_kernel,
            out_shape=jax.ShapeDtypeStruct((size, *array.shape), array.dtype),
            in_specs=[pl.BlockSpec(memory_space=pltpu.HBM)],
            out_specs=vmem(),
            scratch_shapes=[
                pltpu.VMEM(array.shape, array.dtype),
                pltpu.SemaphoreType.DMA,
            ],
            compiler_params=grant(2),
        )(pltpu.with_memory_space_constraint(array, pltpu.HBM)),
        axes,
        0,
        0,
        tiled=True,
    )


def shards(out, back, vectors, tiles, tile_rows, tile_cols, tile_count):
    axes = ("row", "col")
    n_row, n_col = lax.axis_size("row"), lax.axis_size("col")
    vecs, slots = vectors.shape[0], tiles.shape[0]
    pieces = n_col // 2
    row_index, col_index = lax.axis_index("row"), lax.axis_index("col")
    core, side = row_index % 2, col_index % 2
    swap = [(r, r ^ 1) for r in range(n_row)]

    col_place = ((tile_cols // n_col) ^ core) * n_col + tile_cols % n_col
    nothing = 2 * n_col
    live = jnp.arange(slots, dtype=jnp.int32) < tile_count[0]
    mirrored = live & ((row_index != col_index % n_row) | (tile_rows != tile_cols))
    mirror_source = jnp.where(mirrored, tile_rows, nothing)
    plain_source = jnp.where(live, col_place, nothing)

    own = spread(vectors, "col")
    mine = lax.dynamic_slice_in_dim(own, side * pieces, pieces, 0)
    mine = lax.ppermute(mine, axes, out)
    keep, give = products(True, tile_count, mirror_source, col_place, [own], tiles)
    came = lax.ppermute(give, "row", swap)
    sums = join(keep, came)
    sums = lax.ppermute(sums, axes, back)

    theirs = lax.ppermute(mine, "row", swap)
    plain = products(False, tile_count, plain_source, tile_rows, [mine, theirs], tiles)
    plain = merge(side[None].astype(jnp.int32), plain, sums)
    plain = lax.all_to_all(plain, "col", 0, 0, tiled=True)
    return total(vecs, plain)


def solution(mesh):
    sizes = mesh.shape["row"], mesh.shape["col"]
    out = handing(TAKERS_OUT, *sizes)
    back = [(taker, giver) for giver, taker in handing(TAKERS_BACK, *sizes)]

    def step(*args):
        return shards(out, back, *args)

    both = ("row", "col")
    return jax.shard_map(
        step,
        mesh=mesh,
        in_specs=(P(None, both), P(both, None, None), P(both), P(both), P(both)),
        out_specs=P(None, both),
        check_vma=False,
    )
```

```python
import functools

import jax
import jax.numpy as jnp
from jax import lax
from jax.experimental import pallas as pl
from jax.experimental.pallas import tpu as pltpu
from jax.sharding import PartitionSpec as P

CHUNK = 16
GROUP = 8
TOP = 14
TAKERS = (
    (8, 5, 4, 27, 20, 31, 34, 47, 46, 39, 38, 9, 12, 1, 24, 25, 28, 21, 16, 35, 44, 33, 0, 13, 6, 7, 18, 29, 30, 17, 32, 41, 40, 37, 36, 11, 10, 15, 14, 19, 22, 23, 26, 43, 42, 45, 2, 3),
    (8, 13, 0, 1, 16, 25, 30, 35, 38, 47, 42, 5, 4, 9, 12, 17, 24, 29, 28, 21, 36, 43, 34, 33, 2, 15, 6, 7, 20, 23, 26, 37, 44, 45, 40, 41, 14, 11, 10, 31, 18, 27, 22, 19, 32, 39, 46, 3),
    (6, 11, 10, 7, 2, 25, 28, 17, 40, 41, 44, 37, 32, 15, 14, 3, 22, 27, 26, 23, 30, 33, 36, 39, 34, 9, 0, 1, 18, 19, 24, 31, 46, 43, 42, 47, 12, 13, 8, 5, 4, 21, 20, 29, 16, 45, 38, 35),
    (44, 3, 10, 11, 6, 7, 18, 27, 20, 33, 40, 41, 42, 39, 2, 15, 14, 19, 30, 31, 26, 23, 34, 45, 38, 47, 4, 5, 8, 1, 16, 25, 22, 35, 46, 43, 32, 9, 0, 13, 12, 29, 28, 21, 24, 17, 36, 37),
    (46, 43, 8, 13, 12, 5, 4, 23, 18, 19, 42, 47, 34, 39, 38, 1, 0, 9, 16, 17, 28, 29, 24, 35, 40, 41, 44, 11, 10, 3, 20, 21, 22, 25, 36, 37, 32, 33, 6, 7, 14, 15, 2, 31, 30, 27, 26, 45),
    (38, 47, 46, 35, 12, 13, 8, 9, 26, 27, 30, 39, 42, 43, 34, 5, 4, 1, 0, 25, 24, 17, 28, 29, 44, 37, 36, 3, 6, 11, 2, 7, 16, 19, 20, 21, 40, 45, 32, 41, 10, 15, 14, 23, 22, 31, 18, 33),
    (36, 45, 44, 33, 32, 15, 14, 3, 10, 23, 26, 19, 22, 41, 40, 37, 6, 7, 2, 11, 18, 31, 30, 27, 34, 35, 46, 39, 38, 5, 8, 1, 4, 21, 16, 17, 24, 47, 42, 43, 0, 9, 12, 13, 20, 25, 28, 29),
    (24, 33, 32, 45, 44, 37, 10, 15, 2, 7, 16, 29, 30, 31, 36, 41, 40, 11, 6, 3, 14, 27, 18, 19, 26, 39, 38, 43, 46, 47, 4, 5, 0, 1, 22, 23, 20, 21, 34, 35, 42, 9, 8, 13, 12, 17, 28, 25),
    (18, 19, 26, 35, 38, 39, 34, 1, 0, 5, 4, 23, 22, 21, 42, 47, 46, 43, 12, 9, 8, 13, 24, 25, 16, 17, 20, 37, 44, 41, 40, 15, 14, 7, 28, 29, 30, 27, 36, 33, 32, 45, 6, 11, 2, 3, 10, 31),
    (26, 23, 18, 39, 34, 35, 46, 43, 0, 1, 12, 27, 28, 31, 24, 25, 42, 47, 38, 13, 4, 5, 8, 9, 20, 17, 16, 29, 32, 45, 36, 33, 10, 15, 6, 21, 22, 19, 30, 41, 40, 37, 44, 3, 2, 11, 14, 7),
    (16, 29, 24, 25, 20, 33, 40, 41, 44, 3, 6, 7, 10, 21, 22, 27, 36, 45, 32, 37, 14, 11, 2, 15, 30, 31, 18, 19, 26, 43, 38, 39, 46, 9, 8, 13, 4, 17, 28, 23, 42, 47, 34, 35, 12, 5, 0, 1),
    (2, 11, 20, 21, 24, 25, 32, 33, 40, 41, 14, 15, 6, 3, 28, 29, 30, 23, 44, 45, 36, 37, 10, 7, 12, 27, 22, 19, 18, 31, 46, 47, 42, 43, 8, 9, 0, 1, 26, 17, 16, 35, 38, 39, 34, 13, 4, 5),
    (14, 9, 30, 23, 26, 19, 42, 43, 46, 47, 38, 11, 0, 1, 12, 27, 22, 29, 20, 39, 34, 35, 4, 5, 8, 13, 28, 17, 24, 25, 16, 41, 32, 33, 44, 15, 10, 3, 2, 21, 18, 31, 40, 37, 36, 45, 6, 7),
    (12, 3, 6, 31, 18, 27, 22, 47, 38, 43, 34, 35, 8, 5, 4, 1, 30, 23, 26, 29, 42, 39, 46, 13, 0, 9, 10, 25, 16, 21, 20, 17, 44, 41, 32, 33, 2, 7, 14, 15, 24, 19, 28, 45, 40, 37, 36, 11),
    (40, 1, 0, 11, 28, 21, 20, 29, 32, 37, 36, 33, 6, 3, 2, 7, 10, 27, 24, 31, 30, 45, 44, 41, 14, 13, 8, 15, 26, 19, 22, 23, 18, 39, 38, 47, 42, 5, 4, 9, 12, 17, 16, 25, 46, 43, 34, 35),
    (36, 41, 10, 1, 0, 29, 20, 21, 28, 45, 32, 37, 44, 11, 6, 7, 2, 3, 30, 25, 16, 27, 40, 33, 38, 15, 14, 9, 4, 23, 18, 19, 22, 31, 46, 39, 34, 47, 12, 5, 8, 13, 26, 17, 24, 35, 42, 43),
)


def grant(mib):
    return pltpu.CompilerParams(vmem_limit_bytes=mib * 2**20)


def vmem():
    return pl.BlockSpec(memory_space=pltpu.VMEM)


def powers(exponent):
    low = exponent >> 1
    return (
        jnp.exp2(low.astype(jnp.float32)),
        jnp.exp2((exponent - low).astype(jnp.float32)),
    )


def pack(sums, payload, at):
    group, _, rows, width = sums.shape
    half = rows // 2
    peak = jnp.max(jnp.max(jnp.abs(sums), axis=1), axis=-1, keepdims=True)
    peak = jnp.maximum(peak, 1.2e-38)
    exponent = jnp.floor(jnp.log2(peak)).astype(jnp.int32)
    first, second = powers(TOP - exponent)
    for s in range(2):
        scaled = jnp.round((sums[:, s] * first) * second)
        scaled = jnp.minimum(jnp.maximum(scaled, -32767.0), 32767.0)
        scaled = scaled.astype(jnp.int32).astype(jnp.int16)
        payload[pl.ds(at, group), s * rows : (s + 1) * rows] = scaled
    lane = lax.broadcasted_iota(jnp.int32, (group, half, width), 2)
    both = jnp.where(lane < width // 2, exponent[:, :half], exponent[:, half:])
    payload[pl.ds(at, group), 2 * rows : 2 * rows + half] = both.astype(jnp.int16)


def unpack(payload, at, group, rows):
    half = rows // 2
    width = payload.shape[-1]
    exponent = payload[pl.ds(at, group), 2 * rows : 2 * rows + half].astype(jnp.int32)
    factors = []
    for factor in powers(exponent - TOP):
        upper = jnp.broadcast_to(factor[:, :, :1], (group, half, width))
        lower = factor[:, :, width // 2 : width // 2 + 1]
        lower = jnp.broadcast_to(lower, (group, half, width))
        factors.append(jnp.concatenate([upper, lower], axis=1))
    parts = [payload[pl.ds(at, group), s * rows : (s + 1) * rows] for s in range(2)]
    return [(part.astype(jnp.float32) * factors[0]) * factors[1] for part in parts]


def product_kernel(mirror, meta, sources, targets, *refs):
    if mirror:
        own, tiles, keep, give, x, held, sems, acc = refs
        parts = [own]
    else:
        mine, theirs, held, acc, x = refs
        parts = [mine, theirs]
    width = held.shape[1]
    chunks = held.shape[0] // CHUNK

    def copy(step):
        part = pl.ds(step * CHUNK, CHUNK)
        return pltpu.make_async_copy(tiles.at[part], held.at[part], sems.at[step])

    if mirror:
        for step in range(chunks):

            @pl.when(step * CHUNK < meta[0])
            def _(step=step):
                copy(step).start()

    at = 0
    for part in parts:
        size = part.shape[0]
        for s in range(2):
            x[at : at + size, s] = part[:, :, s * width : (s + 1) * width]
        at += size
    x[at] = jnp.zeros(x.shape[1:], x.dtype)
    acc[...] = jnp.zeros_like(acc)

    def step_body(step, carry):
        @pl.when(step * CHUNK < meta[0])
        def _():
            if mirror:
                copy(step).wait()
            found = []
            for u in range(CHUNK):
                k = step * CHUNK + u
                source = sources[k]
                found.append(
                    lax.dot_general(
                        x[source // 2, source % 2],
                        held[k],
                        (((1,), (0 if mirror else 1,)), ((), ())),
                        preferred_element_type=jnp.float32,
                    )
                )
            for u in range(CHUNK):
                target = targets[step * CHUNK + u]
                acc[target // 2, target % 2] += found[u]

        return carry

    lax.fori_loop(0, chunks, step_body, 0)
    if mirror:
        half = keep.shape[0]
        keep[...] = acc[:half]
        give[...] = acc[half:]


def products(mirror, meta, sources, targets, segment, tiles):
    smem = pl.BlockSpec(memory_space=pltpu.SMEM)
    space = pltpu.HBM if mirror else pltpu.VMEM
    tiles = pltpu.with_memory_space_constraint(tiles, space)
    pieces = segment[0].shape[0] * len(segment)
    vecs = segment[0].shape[1]
    width = tiles.shape[1]
    scratch = [pltpu.VMEM((pieces + 1, 2, vecs, width), jnp.bfloat16)]
    if mirror:
        shapes = [jax.ShapeDtypeStruct((pieces // 2, 2, vecs, width), jnp.float32)] * 2
        outs = [vmem(), vmem()]
        scratch += [
            pltpu.VMEM(tiles.shape, tiles.dtype),
            pltpu.SemaphoreType.DMA((tiles.shape[0] // CHUNK,)),
            pltpu.VMEM((pieces, 2, vecs, width), jnp.float32),
        ]
    else:
        shapes = jax.ShapeDtypeStruct((pieces, 2, vecs, width), jnp.float32)
        outs = vmem()
    return pl.pallas_call(
        functools.partial(product_kernel, mirror),
        out_shape=shapes,
        in_specs=[smem] * 3 + [vmem()] * len(segment) + [pl.BlockSpec(memory_space=space)],
        out_specs=outs,
        scratch_shapes=scratch,
        compiler_params=grant(12 if mirror else 4),
    )(meta, sources, targets, *segment, tiles)


def join_kernel(keep, came, payload):
    def body(i, carry):
        part = pl.ds(i * GROUP, GROUP)
        pack(keep[part] + came[part], payload, i * GROUP)
        return carry

    lax.fori_loop(0, payload.shape[0] // GROUP, body, 0)


def join(keep, came):
    pieces, _, vecs, width = keep.shape
    return pl.pallas_call(
        join_kernel,
        out_shape=jax.ShapeDtypeStruct((pieces, 5 * vecs // 2, width), jnp.int16),
        in_specs=[vmem()] * 2,
        out_specs=vmem(),
        compiler_params=grant(4),
    )(keep, came)


def merge_kernel(side, sums, came, payload):
    pieces, _, vecs, _ = sums.shape
    half = pieces // 2
    first, other = side[0] * half, (1 - side[0]) * half

    def body(i, carry):
        at = i * GROUP
        added = jnp.stack(unpack(came, at, GROUP, vecs), axis=1)
        pack(sums[pl.ds(first + at, GROUP)] + added, payload, first + at)
        pack(sums[pl.ds(other + at, GROUP)], payload, other + at)
        return carry

    lax.fori_loop(0, half // GROUP, body, 0)


def merge(side, sums, came):
    pieces, _, vecs, width = sums.shape
    return pl.pallas_call(
        merge_kernel,
        out_shape=jax.ShapeDtypeStruct((pieces, 5 * vecs // 2, width), jnp.int16),
        in_specs=[pl.BlockSpec(memory_space=pltpu.SMEM)] + [vmem()] * 2,
        out_specs=vmem(),
        compiler_params=grant(4),
    )(side, sums, came)


def total_kernel(vecs, payload, out):
    width = payload.shape[-1]

    def body(i, sums):
        parts = unpack(payload, i * GROUP, GROUP, vecs)
        return tuple(one + part.sum(axis=0) for one, part in zip(sums, parts))

    zero = jnp.zeros((vecs, width), jnp.float32)
    sums = lax.fori_loop(0, payload.shape[0] // GROUP, body, (zero, zero))
    for s in range(2):
        out[:, s * width : (s + 1) * width] = sums[s]


def total(vecs, payload):
    return pl.pallas_call(
        functools.partial(total_kernel, vecs),
        out_shape=jax.ShapeDtypeStruct((vecs, 2 * payload.shape[-1]), jnp.float32),
        in_specs=[vmem()],
        out_specs=vmem(),
        compiler_params=grant(4),
    )(payload)


def handing(n_row, n_col):
    pairs = []
    for m in range(n_row):
        takers = [(r, c) for c in range(m, n_col, n_row) for r in range(n_row)]
        for c, taker in enumerate(TAKERS[m]):
            r, col = takers[taker]
            pairs.append((m * n_col + c, r * n_col + col))
    return pairs


def copies_kernel(array, out):
    out[...] = jnp.broadcast_to(array[...][None], out.shape)


def spread(array, axes):
    copies = pl.pallas_call(
        copies_kernel,
        out_shape=pltpu.VMEM((lax.axis_size(axes), *array.shape), array.dtype),
        in_specs=[vmem()],
        out_specs=vmem(),
        compiler_params=grant(2),
    )(array)
    return lax.all_to_all(copies, axes, 0, 0, tiled=True)


def shards(pairs, vectors, tiles, tile_rows, tile_cols, tile_count):
    axes = ("row", "col")
    n_row, n_col = lax.axis_size("row"), lax.axis_size("col")
    vecs, slots = vectors.shape[0], tiles.shape[0]
    pieces = n_col // 2
    row_index, col_index = lax.axis_index("row"), lax.axis_index("col")
    core, side = row_index % 2, col_index % 2
    swap = [(r, r ^ 1) for r in range(n_row)]

    col_place = ((tile_cols // n_col) ^ core) * n_col + tile_cols % n_col
    nothing = 2 * n_col
    live = jnp.arange(slots, dtype=jnp.int32) < tile_count[0]
    mirrored = live & ((row_index != col_index % n_row) | (tile_rows != tile_cols))
    mirror_source = jnp.where(mirrored, tile_rows, nothing)
    plain_source = jnp.where(live, col_place, nothing)

    own = spread(vectors, "col")
    mine = lax.dynamic_slice_in_dim(own, side * pieces, pieces, 0)
    mine = lax.ppermute(mine, axes, pairs)
    keep, give = products(True, tile_count, mirror_source, col_place, [own], tiles)
    came = lax.ppermute(give, "row", swap)
    sums = join(keep, came)
    sums = lax.ppermute(sums, axes, [(taker, giver) for giver, taker in pairs])

    theirs = lax.ppermute(mine, "row", swap)
    plain = products(False, tile_count, plain_source, tile_rows, [mine, theirs], tiles)
    plain = merge(side[None].astype(jnp.int32), plain, sums)
    plain = lax.all_to_all(plain, "col", 0, 0, tiled=True)
    return total(vecs, plain)


def solution(mesh):
    pairs = handing(mesh.shape["row"], mesh.shape["col"])

    def step(*args):
        return shards(pairs, *args)

    both = ("row", "col")
    return jax.shard_map(
        step,
        mesh=mesh,
        in_specs=(P(None, both), P(both, None, None), P(both), P(both), P(both)),
        out_specs=P(None, both),
        check_vma=False,
    )
```
